32 devices in a mesh: groups: 2 (over x), req: 8 (over z, y), head: 2 (over core).
Axes of the slice: x: 2, y: 2, z: 4, core: 2. Of those that a mesh axis runs over, the one named last changes fastest.
Arguments:
- queries: bfloat16 [2048, 32, 128], P(('groups', 'req'), 'head'), parts along dimension 0, may hold values from -100 to 100
- new_keys: bfloat16 [2048, 2, 128], P(('groups', 'req'), 'head'), parts along dimension 0, may hold values from -4.5 to 4.5
- new_values: bfloat16 [2048, 2, 128], P(('groups', 'req'), 'head'), parts along dimension 0, may hold values from -6 to 6
- cluster_kv: bfloat16 [1024, 2, 2, 128, 128], P(('groups', 'req'), 'head'), parts along dimension 0, may hold values from -6 to 6
- cluster_len: int32 [32], P('groups'), parts along dimension 0, may hold values from 1 to 4096, 40960 in all
- piece_slot: int32 [32, 32], P('groups'), parts along dimension 0, may hold values from 0 to 511, as said below
- cluster_ids: int32 [16, 2, 2], P('groups', 'head'), parts along dimension 0, may hold values from 0 to 15, all different within a row
- w_out: bfloat16 [4096, 4096], P('head', 'req'), may hold values from -0.09375 to 0.09375
Outputs:
- projected: bfloat16 [2048, 4096], P(('groups', 'req', 'head')), parts along dimension 0
The draws below stay inside these ranges and needn't reach their ends.
There are 2 independent parts, one for each index of `groups`. The reference program is written for one: setup_inputs(seed, part) draws one part's arguments, and reference() takes and returns one part's arrays. A program takes and returns all parts, laid end to end along the dimension named above; an argument that names none is the same for every part. Nothing has to cross between parts.
Inputs may be any that keep to these rules, and one draw needn't show every extreme that they name: `cluster_ids`: for each request and KV head, 2 distinct cluster numbers. A permutation of the slots: piece p of cluster c lies in slot piece_slot[c, p], stored on index slot // 64 of req, and every cluster has exactly 4 of its pieces on every index of req.
All inputs are finite; a program needn't handle non-finite values.
Results may differ from the reference program's by a relative error of at most 0.0052.
Values may be sent and summed in bfloat16 or wider, within the bound.
A program may use at most 128 MiB of HBM per device.

```python
import math
import jax
import jax.numpy as jnp
import numpy as np
from jax import lax

D = 4096
HD = 128
QH = 32
KVH = 2
PIECE = 128
PCS = 32
NCL_DEV = 2
SEL = 2
TOK = 128
CL = 4096
NCL = 16
N_REQ = 8


def shared_keys(key):
    normal_keys = jax.random.normal(jax.random.fold_in(key, 7), (N_REQ * TOK, KVH, HD), jnp.float32)
    return jnp.clip(normal_keys, -4.5, 4.5)


def draw_new_keys(key, part):
    return shared_keys(key).astype(jnp.bfloat16)


def draw_queries(key, part):
    first_key = jax.random.fold_in(key, 13)
    second_key = jax.random.fold_in(key, 17)
    shape = (N_REQ * TOK, QH, HD)
    base = jax.random.normal(first_key, shape, jnp.float32)
    scales = jnp.exp(jax.random.uniform(second_key, (N_REQ * TOK, QH, 1), jnp.float32, -0.7, 1.1))
    result = base * scales
    return jnp.clip(result, -100.0, 100.0).astype(jnp.bfloat16)


def draw_piece_slot(key, part):
    per_peer = PCS // N_REQ
    held_slots = NCL_DEV * PCS
    first_scores = jax.random.randint(jax.random.fold_in(key, 41), (NCL, PCS), 0, 1 << 20) * PCS + jnp.arange(PCS, dtype=jnp.int32)[None, :]
    position = jnp.argsort(first_scores, axis=1).astype(jnp.int32)
    owner_index = position % N_REQ
    within = position // N_REQ
    second_scores = jax.random.randint(jax.random.fold_in(key, 42), (N_REQ, held_slots), 0, 1 << 20) * held_slots + jnp.arange(held_slots, dtype=jnp.int32)[None, :]
    device_perm = jnp.argsort(second_scores, axis=1).astype(jnp.int32)
    entry = jnp.arange(NCL, dtype=jnp.int32)[:, None] * per_peer + within
    local_slot = device_perm[owner_index, entry]
    return (owner_index * held_slots + local_slot).astype(jnp.int32)


def block_levels(key, extent, pieces, least, high):
    factor_of, own = 1.0, jax.random.fold_in(key, 6)
    for dim, parts in pieces:
        draws = jnp.exp(jax.random.uniform(jax.random.fold_in(own, dim), (parts,), jnp.float32, least / len(pieces), high / len(pieces)))
        factor_of = factor_of * jnp.repeat(draws, extent[dim] // parts).reshape([-1 if axis == dim else 1 for axis in range(len(extent))])
    return factor_of


def different_ones(stream_key, rows, count, top, lift):
    sequence = jax.random.permutation(jax.random.fold_in(stream_key, 1), count)
    boost = sequence
    for power in range(3):
        boost = boost * boost // count
    boost = boost * lift // count
    lots = jax.random.randint(jax.random.fold_in(stream_key, 2), (rows, count), 0, 4096) + boost
    fixed_rows = jax.random.permutation(jax.random.fold_in(stream_key, 3), rows)[jnp.arange(count) % rows]
    lots = jnp.where(jnp.arange(rows)[:, None] == fixed_rows[None, :], 1 << 14, lots)
    priority = lots * count + jnp.arange(count)
    return lax.top_k(priority.astype(jnp.int32), top)[1].astype(jnp.int32)


def length_profile(number_of, total, reach, skew):
    weights = [(1 << 20) // math.isqrt(standing ** skew) + 1 for standing in range(2, number_of + 1)]
    spare, counts = total - reach - (number_of - 1), [1] * (number_of - 1)
    while spare > 0:
        candidates = [i for i in range(number_of - 1) if counts[i] < reach]
        whole, remaining = sum([weights[i] for i in candidates]), spare
        for i in candidates:
            extra = min(reach - counts[i], max(1, remaining * weights[i] // whole), spare)
            counts[i] = counts[i] + extra
            spare = spare - extra
    return np.array([reach] + counts)


def ragged_sizes(key, count, total, limit, lean):
    if count == 2:
        one = jax.random.randint(key, (), max(1, total - limit), min(limit, total - 1) + 1)
        return jnp.stack([one, total - one])
    sizes = jnp.asarray(length_profile(count, total, limit, lean), jnp.int32)
    twos = (count - 1) // 2
    source_of, receiver = sizes[1:1 + 2 * twos:2], sizes[2:2 + 2 * twos:2]
    margin = jnp.minimum(source_of - 1, limit - receiver)
    passed = jax.random.randint(jax.random.fold_in(key, 1), (twos,), 0, 1 << 20) % (margin + 1)
    sizes = sizes.at[1:1 + 2 * twos:2].set(source_of - passed).at[2:2 + 2 * twos:2].set(receiver + passed)
    return sizes[jax.random.permutation(jax.random.fold_in(key, 2), count)]


def bell_draw(rng, extent, spread, reach, split=(), held_as=jnp.bfloat16):
    array = jax.random.normal(rng, extent, jnp.float32) * spread
    if len(split) > 0:
        array = block_levels(rng, extent, split, -0.22, 0.18) * array
    return jnp.clip(array, min=-reach, max=reach).astype(held_as)


def setup_inputs(seed: int = 0, part: int = 0) -> dict:
    streams_of = jax.random.split(jax.random.key(seed), 9)
    part_splits = jax.random.split(jax.random.fold_in(streams_of[8], part), 9)
    queries = draw_queries(jax.random.fold_in(jax.random.fold_in(streams_of[8], part), 71), part)
    new_keys = draw_new_keys(jax.random.fold_in(jax.random.fold_in(streams_of[8], part), 71), part)
    new_values = bell_draw(part_splits[2], (N_REQ * TOK, KVH, HD), 1.0, 6.0, ((0, 8), (1, 2)))
    cluster_kv = bell_draw(part_splits[3], (NCL * PCS, KVH, 2, PIECE, HD), 1.0, 6.0, ((0, 8), (1, 2)))
    cluster_len = ragged_sizes(part_splits[4], NCL, NCL * CL * 5 // 8, CL, 1).astype(jnp.int32)
    piece_slot = draw_piece_slot(jax.random.fold_in(jax.random.fold_in(streams_of[8], part), 71), part)
    cluster_ids = different_ones(part_splits[6], N_REQ * KVH, NCL, SEL, 1024).reshape((N_REQ, KVH, SEL))
    w_out = bell_draw(streams_of[7], (QH * HD, D), (QH * HD) ** -0.5, 0.09375, ((0, 2), (1, 8)))
    return {"queries": queries, "new_keys": new_keys, "new_values": new_values, "cluster_kv": cluster_kv, "cluster_len": cluster_len, "piece_slot": piece_slot, "cluster_ids": cluster_ids, "w_out": w_out}


def reference(queries, new_keys, new_values, cluster_kv, cluster_len, piece_slot, cluster_ids, w_out):
    group_size = QH // KVH
    scale_factor = HD ** -0.5
    position = jnp.arange(TOK, dtype=jnp.int32)
    causal = position[:, None] >= position[None, :]
    key_offset = (jnp.arange(PCS, dtype=jnp.int32)[:, None] * PIECE + jnp.arange(PIECE, dtype=jnp.int32)[None, :]).reshape(CL)

    def per_request(request):
        start_row = (request * TOK).astype(jnp.int32)
        query_rows = lax.dynamic_slice_in_dim(queries, start_row, TOK, 0)
        key_rows = lax.dynamic_slice_in_dim(new_keys, start_row, TOK, 0)
        value_rows = lax.dynamic_slice_in_dim(new_values, start_row, TOK, 0)
        plan_row = lax.dynamic_index_in_dim(cluster_ids, request, 0, keepdims=False)
        outputs = []
        for group_index in range(KVH):
            chosen = plan_row[group_index]
            slot_rows = piece_slot[chosen].reshape(SEL * PCS)
            picked = cluster_kv[slot_rows, group_index]
            lengths = cluster_len[chosen]
            valid_keys = (key_offset[None, :] < lengths[:, None]).reshape(SEL * CL)
            cached_keys = picked[:, 0].reshape(SEL * CL, HD).astype(jnp.float32)
            cached_values = picked[:, 1].reshape(SEL * CL, HD).astype(jnp.float32)
            own_keys = key_rows[:, group_index].astype(jnp.float32)
            own_values = value_rows[:, group_index].astype(jnp.float32)
            query_group = query_rows[:, group_index * group_size:(group_index + 1) * group_size].astype(jnp.float32)
            cached_scores = jnp.einsum("thd,kd->htk", query_group, cached_keys) * scale_factor
            cached_scores = jnp.where(valid_keys[None, None, :], cached_scores, -jnp.inf)
            own_scores = jnp.einsum("thd,ud->htu", query_group, own_keys) * scale_factor
            own_scores = jnp.where(causal[None], own_scores, -jnp.inf)
            row_top = jnp.maximum(jnp.max(cached_scores, axis=2), jnp.max(own_scores, axis=2))
            cached_weights = jnp.exp(cached_scores - row_top[:, :, None])
            own_weights = jnp.exp(own_scores - row_top[:, :, None])
            row_total = jnp.sum(cached_weights, axis=2) + jnp.sum(own_weights, axis=2)
            cached_low = cached_weights.astype(jnp.bfloat16).astype(jnp.float32)
            own_low = own_weights.astype(jnp.bfloat16).astype(jnp.float32)
            mixed_sum = jnp.einsum("htk,kd->htd", cached_low, cached_values) + jnp.einsum("htu,ud->htd", own_low, own_values)
            result = (mixed_sum / row_total[:, :, None]).astype(jnp.bfloat16)
            outputs.append(jnp.transpose(result, (1, 0, 2)))
        return jnp.concatenate(outputs, axis=1).reshape(TOK, QH * HD)

    attended = lax.map(per_request, jnp.arange(N_REQ, dtype=jnp.int32)).reshape(N_REQ * TOK, QH * HD)
    return jnp.dot(attended, w_out, preferred_element_type=jnp.float32).astype(jnp.bfloat16)
```

```python
import functools

import jax
import jax.numpy as jnp
from jax import lax
from jax.experimental import pallas as pl
from jax.experimental.pallas import tpu as pltpu
from jax.sharding import PartitionSpec as P

MESH = pl.DeviceIdType.MESH
NEG = -1e30
LOG2E = 1.4426950408889634


def pick_kernel(far, ids_ref, slot_ref, len_ref, kv_ref, q_ref, send_ref, lim_ref, idx_ref, qt_ref,
                pick, held_pieces, in_sem, out_sem):
    me = lax.axis_index("req")
    lo = me % 2
    held, _, _, piece_keys, _ = kv_ref.shape
    sel = ids_ref.shape[2]
    pieces = slot_ref.shape[1]
    per = pieces // (2 * far)
    base = me * held
    other = (me + 1 - 2 * lo) * held

    @pl.loop(0, far)
    def _(z):
        for s in range(sel):
            c = ids_ref[z * 2 + 1 - lo, 0, s]
            n = jnp.int32(0)
            for p in range(pieces):
                loc = slot_ref[c, p] - base
                pick[n] = loc
                n = n + ((loc >= 0) & (loc < held)).astype(jnp.int32)
            for j in range(per):
                pltpu.make_async_copy(kv_ref.at[pick[j], 0], held_pieces.at[z, s * per + j], in_sem.at[z]).start()

    groups, _, cols = qt_ref.shape
    tok, heads, _ = q_ref.shape
    per_group = heads // groups
    for h in range(heads):
        at = h % per_group
        qt_ref[h // per_group, :, at * tok:(at + 1) * tok] = q_ref[:, h, :].T

    @pl.loop(0, far)
    def _(z):
        pltpu.make_async_copy(send_ref.at[z], held_pieces.at[z], in_sem.at[z]).wait()
        pltpu.make_async_copy(held_pieces.at[z], send_ref.at[z], out_sem.at[z]).start()

    @pl.loop(0, far)
    def _(z):
        for s in range(sel):
            c = ids_ref[z * 2 + lo, 0, s]
            fill = len_ref[c]
            n = jnp.int32(s * per)
            k = jnp.int32(s * per)
            for p in range(pieces):
                slot = slot_ref[c, p]
                loc = slot - base
                away = slot - other
                left = fill - p * piece_keys
                idx_ref[z, n] = loc
                lim_ref[0, z, n] = left
                n = n + ((loc >= 0) & (loc < held)).astype(jnp.int32)
                lim_ref[1, z, k] = left
                k = k + ((away >= 0) & (away < held)).astype(jnp.int32)

    @pl.loop(0, far)
    def _(z):
        pltpu.make_async_copy(held_pieces.at[z], send_ref.at[z], out_sem.at[z]).wait()


def serve_kernel(far, lim_ref, idx_ref, send_ref, q_ref, k_ref, v_ref, kv_ref, w_ref, out_ref,
                 nbr, qt, kb, vb, top, total, acc, mine, mine_st, came, came_st, full, wv, part, got, low,
                 load_sem, kv_send, kv_recv, q_send, q_recv, p_send, p_recv, s_send, s_recv, a_send, a_recv,
                 wy_send, wy_recv, wx_send, wx_recv, part_send, part_recv, out_send, out_recv):
    me = lax.axis_index("req")
    head = lax.axis_index("head")
    grp = lax.axis_index("groups")
    hi, lo = me // 2, me % 2
    end = far - 1
    pair = {"req": me + 1 - 2 * lo}
    twin = {"groups": grp + 1 - 2 * (grp % 2)}
    mate = {"head": 1 - head}

    tok, hd = k_ref.shape
    count, piece_keys = send_ref.shape[1], send_ref.shape[3]
    keys = count * piece_keys
    groups, _, cols = q_ref.shape
    per_group = cols // tok
    block = min(128, cols)
    factor = hd ** (-0.5) * LOG2E
    half = out_ref.shape[0]
    depth, columns = w_ref.shape
    wide = 2 * columns
    slab = depth // (2 * groups)
    slice_depth = depth // groups

    def at(z):
        return {"req": z * 2 + lo}

    load_q = pltpu.make_async_copy(q_ref, qt.at[hi], load_sem.at[0])
    load_w = pltpu.make_async_copy(w_ref, wv.at[lo], load_sem.at[1])
    load_q.start()
    load_w.start()

    barrier = pltpu.get_barrier_semaphore()
    for k in range(1, far):
        pl.semaphore_signal(barrier, inc=1, device_id=at(lax.rem(hi + k, far)), device_id_type=MESH)
    for device in (pair, twin, mate):
        pl.semaphore_signal(barrier, inc=1, device_id=device, device_id_type=MESH)
    pl.semaphore_wait(barrier, far + 2)

    shorter = jnp.where(hi < end - hi, hi, end - hi)

    def order(i):
        both = i <= 2 * shorter
        d = jnp.where(both, (i + 1) // 2, i - shorter)
        above = jnp.where(both, i % 2 == 1, hi < end - hi)
        return jnp.where(i == far, hi, jnp.where(above, hi + d, hi - d))

    def q_copy(z, g, to, way):
        return pltpu.make_async_remote_copy(
            src_ref=qt.at[z, g], dst_ref=qt.at[z, g], send_sem=q_send.at[way, z, g],
            recv_sem=q_recv.at[z, g], device_id=at(to), device_id_type=MESH)

    def a_copy(z, g, to, way):
        return pltpu.make_async_remote_copy(
            src_ref=full.at[z, g], dst_ref=full.at[z, g], send_sem=a_send.at[way, z, g],
            recv_sem=a_recv.at[z, g], device_id=at(to), device_id_type=MESH)

    def kv_copy(z):
        return pltpu.make_async_remote_copy(
            src_ref=send_ref.at[z], dst_ref=nbr.at[z], send_sem=kv_send.at[z],
            recv_sem=kv_recv.at[z], device_id=pair, device_id_type=MESH)

    def w_rows(which, c):
        return pl.ds(pl.multiple_of((which * groups + c) * slab, slab), slab)

    def wy_copy(c, slot):
        rows = w_rows(grp % 2, c)
        return pltpu.make_async_remote_copy(
            src_ref=w_ref.at[rows], dst_ref=wv.at[slot, rows], send_sem=wy_send.at[c],
            recv_sem=wy_recv.at[c], device_id=pair, device_id_type=MESH)

    def wx_copy(c, which):
        rows = w_rows(which, c)
        return pltpu.make_async_remote_copy(
            src_ref=wv.at[1 - lo, rows], dst_ref=wv.at[1 - lo, rows], send_sem=wx_send.at[c],
            recv_sem=wx_recv.at[c], device_id=twin, device_id_type=MESH)

    def inner(b):
        return jnp.where(hi > b, hi - 1, hi + 1)

    def part_pair(b, g, slot, to):
        return (
            pltpu.make_async_remote_copy(
                src_ref=mine.at[b, g], dst_ref=came.at[slot, g], send_sem=p_send.at[b, g],
                recv_sem=p_recv.at[slot, g], device_id=at(to), device_id_type=MESH),
            pltpu.make_async_remote_copy(
                src_ref=mine_st.at[b, g], dst_ref=came_st.at[slot, g], send_sem=s_send.at[b, g],
                recv_sem=s_recv.at[slot, g], device_id=at(to), device_id_type=MESH))

    def part_start(b, g):
        to = inner(b)
        slot = jnp.where((to == b) & (hi > b), far, b)
        for copy in part_pair(b, g, slot, to):
            copy.start()

    def part_wait(b, g, slot):
        for copy in part_pair(b, g, slot, jnp.where(hi < end, hi + 1, hi - 1)):
            copy.wait_recv()

    load_q.wait()

    @pl.loop(0, groups)
    def _(g):
        @pl.when(hi < end)
        def _():
            q_copy(hi, g, hi + 1, 0).start()

        @pl.when(hi > 0)
        def _():
            q_copy(hi, g, hi - 1, 1).start()

    @pl.loop(1, far + 1)
    def _(i):
        kv_copy(order(i)).start()

    @pl.loop(0, groups)
    def _(c):
        wy_copy(c, lo).start()

    own_vt = v_ref[...].T
    own_k = k_ref[...]

    @pl.loop(0, groups)
    def _(g):
        s = jnp.dot(own_k, qt[hi, g], preferred_element_type=jnp.float32)
        u = lax.broadcasted_iota(jnp.int32, s.shape, 0)
        t = lax.broadcasted_iota(jnp.int32, s.shape, 1) % tok
        s = jnp.where(u <= t, s, NEG)
        m = jnp.max(s, axis=0, keepdims=True)
        w = jnp.exp2((s - m) * factor)
        top[0, g] = m
        total[0, g] = jnp.sum(w, axis=0, keepdims=True)
        acc[0, g] = jnp.dot(own_vt, w.astype(jnp.bfloat16), preferred_element_type=jnp.float32)

    def unit(z, src, slot, g):
        fills = [lim_ref[src, z, i] for i in range(count)]
        key = lax.broadcasted_iota(jnp.int32, (piece_keys, block), 0)

        def score(b):
            s = jnp.dot(kb[src], qt[z, g, :, b * block:(b + 1) * block], preferred_element_type=jnp.float32)
            return jnp.concatenate(
                [jnp.where(key < fills[i], s[i * piece_keys:(i + 1) * piece_keys], NEG) for i in range(count)], axis=0)

        def weigh(b, s):
            at_b = slice(b * block, (b + 1) * block)
            m_old = top[slot, g, :, at_b]
            m = jnp.maximum(m_old, jnp.max(s, axis=0, keepdims=True))
            keep = jnp.exp2((m_old - m) * factor)
            w = jnp.exp2((s - m) * factor)
            mixed = jnp.dot(vb[src], w.astype(jnp.bfloat16), preferred_element_type=jnp.float32)
            top[slot, g, :, at_b] = m
            total[slot, g, :, at_b] = total[slot, g, :, at_b] * keep + jnp.sum(w, axis=0, keepdims=True)
            acc[slot, g, :, at_b] = acc[slot, g, :, at_b] * keep + mixed

        s = score(0)
        for b in range(cols // block):
            ahead = score(b + 1) if b + 1 < cols // block else None
            weigh(b, s)
            s = ahead

    def blend(m1, l1, a1, m2, l2, a2):
        m = jnp.maximum(m1, m2)
        f1 = jnp.exp2((m1 - m) * factor)
        f2 = jnp.exp2((m2 - m) * factor)
        return m, l1 * f1 + l2 * f2, a1 * f1 + a2 * f2

    def merge(b, g):
        part_wait(b, g, b)
        m, l, a = blend(
            mine_st[b, g, 0:1], mine_st[b, g, 1:2], mine[b, g].astype(jnp.float32),
            came_st[b, g, 0:1], came_st[b, g, 1:2], came[b, g].astype(jnp.float32))
        mine_st[b, g, 0:1] = m
        mine_st[b, g, 1:2] = l
        mine[b, g] = a.astype(jnp.bfloat16)
        part_start(b, g)

    def absorb(slot, g):
        part_wait(hi, g, slot)
        m, l, a = blend(
            top[0, g], total[0, g], acc[0, g],
            came_st[slot, g, 0:1], came_st[slot, g, 1:2], came[slot, g].astype(jnp.float32))
        top[0, g] = m
        total[0, g] = l
        acc[0, g] = a

    last = jnp.where(2 * shorter >= 2 * end - far, far, 2 * (end - shorter))

    @pl.loop(0, 2 * end + 1)
    def _(i):
        b = order(i)
        slot = jnp.where(b == hi, 0, 1)

        @pl.when(i < far)
        def _():
            for j in range(count):
                at_j = slice(j * piece_keys, (j + 1) * piece_keys)
                loc = idx_ref[b, j]
                kb[0, at_j] = kv_ref[loc, 0, 0]
                vb[0, :, at_j] = kv_ref[loc, 0, 1].T

            @pl.when(i > 0)
            def _():
                top[1] = jnp.full_like(top[1], NEG)
                total[1] = jnp.zeros_like(total[1])
                acc[1] = jnp.zeros_like(acc[1])

            @pl.loop(0, groups)
            def _(g):
                @pl.when((i > 0) & (hi - i >= 0))
                def _():
                    q_copy(hi - i, g, hi, 0).wait_recv()

                    @pl.when(hi < end)
                    def _():
                        q_copy(hi - i, g, hi + 1, 0).start()

                @pl.when((i > 0) & (hi + i <= end))
                def _():
                    q_copy(hi + i, g, hi, 1).wait_recv()

                    @pl.when(hi > 0)
                    def _():
                        q_copy(hi + i, g, hi - 1, 1).start()

                unit(b, 0, slot, g)

        @pl.when((i > 0) & (i <= far))
        def _():
            kv_copy(b).wait_recv()
            for j in range(count):
                at_j = slice(j * piece_keys, (j + 1) * piece_keys)
                kb[1, at_j] = nbr[b, j, 0]
                vb[1, :, at_j] = nbr[b, j, 1].T

        @pl.loop(0, groups)
        def _(g):
            @pl.when((i > 0) & (i <= far))
            def _():
                unit(b, 1, slot, g)

                @pl.when(i < far)
                def _():
                    mine_st[b, g, 0:1] = top[1, g]
                    mine_st[b, g, 1:2] = total[1, g]
                    mine[b, g] = acc[1, g].astype(jnp.bfloat16)

                    @pl.when(((hi == end) & (b < hi)) | ((hi == 0) & (b > hi)))
                    def _():
                        part_start(b, g)

            low_b = 2 * end - hi - i
            high_b = i - hi

            @pl.when((low_b >= 0) & (low_b < hi) & (hi < end))
            def _():
                merge(low_b, g)

            @pl.when((high_b > hi) & (high_b <= end) & (hi > 0))
            def _():
                merge(high_b, g)

            @pl.when((i == 2 * hi) & (hi > 0))
            def _():
                absorb(hi, g)

            @pl.when((i == 2 * (end - hi)) & (hi < end))
            def _():
                absorb(far, g)

            @pl.when(i == last)
            def _():
                o = acc[0, g] / total[0, g]
                for h in range(per_group):
                    full[hi, g, :, h * hd:(h + 1) * hd] = o[:, h * tok:(h + 1) * tok].T.astype(full.dtype)

                @pl.when(hi < end)
                def _():
                    a_copy(hi, g, hi + 1, 0).start()

                @pl.when(hi > 0)
                def _():
                    a_copy(hi, g, hi - 1, 1).start()

    def part_copy(z):
        return pltpu.make_async_remote_copy(
            src_ref=part.at[z, 1 - head], dst_ref=got.at[z], send_sem=part_send.at[z],
            recv_sem=part_recv.at[z], device_id=mate, device_id_type=MESH)

    def out_copy(z, owner):
        return pltpu.make_async_remote_copy(
            src_ref=low.at[z], dst_ref=out_ref.at[:, pl.ds(pl.multiple_of(owner * wide, wide), wide)],
            send_sem=out_send.at[z], recv_sem=out_recv.at[owner], device_id=at(z), device_id_type=MESH)

    def compute(z, j):
        at_j = pl.ds(pl.multiple_of(j * columns, columns), columns)
        terms = jnp.dot(full[z, 0], wv[j, 0:slice_depth], preferred_element_type=jnp.float32)
        for g in range(1, groups):
            terms += jnp.dot(full[z, g], wv[j, g * slice_depth:(g + 1) * slice_depth],
                             preferred_element_type=jnp.float32)
        part[z, 0, :, at_j] = terms[:half]
        part[z, 1, :, at_j] = terms[half:]

    def finish(z):
        part_copy(z).wait_recv()
        rows = (part[z, head] + got[z]).astype(out_ref.dtype)

        @pl.when(z == hi)
        def _():
            out_ref[:, pl.ds(pl.multiple_of(hi * wide, wide), wide)] = rows

        @pl.when(z != hi)
        def _():
            low[z] = rows
            out_copy(z, hi).start()

    load_w.wait()
    settle = min(2, end)

    @pl.loop(0, far)
    def _(d):
        @pl.when(d > 0)
        def _():
            @pl.loop(0, 2)
            def _(turn):
                above = (turn == 0) == (hi < end - hi)

                @pl.loop(0, groups)
                def _(g):
                    @pl.when(jnp.logical_not(above) & (hi - d >= 0))
                    def _():
                        a_copy(hi - d, g, hi, 0).wait_recv()

                        @pl.when(hi < end)
                        def _():
                            a_copy(hi - d, g, hi + 1, 0).start()

                    @pl.when(above & (hi + d <= end))
                    def _():
                        a_copy(hi + d, g, hi, 1).wait_recv()

                        @pl.when(hi > 0)
                        def _():
                            a_copy(hi + d, g, hi - 1, 1).start()

                    @pl.when((d == 1) & (turn == 0))
                    def _():
                        wy_copy(g, 1 - lo).wait_recv()
                        wx_copy(g, grp % 2).start()

        @pl.when(d == settle)
        def _():
            @pl.loop(0, groups)
            def _(c):
                wx_copy(c, 1 - grp % 2).wait_recv()

            @pl.loop(0, 2 * settle - 1)
            def _(n):
                z = hi - (settle - 1) + n

                @pl.when((z >= 0) & (z < far))
                def _():
                    compute(z, 1 - lo)
                    part_copy(z).start()

        @pl.loop(0, 2)
        def _(side):
            z = hi + d * (2 * side - 1)

            @pl.when((z >= 0) & (z < far) & ((d > 0) | (side == 0)))
            def _():
                compute(z, lo)

                @pl.when(d >= settle)
                def _():
                    compute(z, 1 - lo)
                    part_copy(z).start()

    @pl.loop(0, far)
    def _(d):
        @pl.loop(0, 2)
        def _(side):
            z = hi + d * (2 * side - 1)

            @pl.when((z >= 0) & (z < far) & ((d > 0) | (side == 0)))
            def _():
                finish(z)

    @pl.loop(0, groups)
    def _(g):
        wy_copy(g, lo).wait_send()
        wx_copy(g, grp % 2).wait_send()

    @pl.loop(0, far)
    def _(z):
        kv_copy(z).wait_send()
        part_copy(z).wait_send()

        @pl.loop(0, groups)
        def _(g):
            @pl.when((z <= hi) & (hi < end))
            def _():
                q_copy(z, g, hi + 1, 0).wait_send()
                a_copy(z, g, hi + 1, 0).wait_send()

            @pl.when((z >= hi) & (hi > 0))
            def _():
                q_copy(z, g, hi - 1, 1).wait_send()
                a_copy(z, g, hi - 1, 1).wait_send()

            @pl.when(z != hi)
            def _():
                for copy in part_pair(z, g, z, inner(z)):
                    copy.wait_send()

        @pl.when(z != hi)
        def _():
            out_copy(z, hi).wait_send()
            out_copy(z, z).wait_recv()


def local(queries, new_keys, new_values, cluster_kv, cluster_len, piece_slot, cluster_ids, w_out):
    peers = lax.axis_size("req")
    far = peers // 2
    tok, heads, hd = queries.shape
    held, _, _, piece_keys, _ = cluster_kv.shape
    pieces = piece_slot.shape[1]
    sel = cluster_ids.shape[2]
    count = sel * (pieces // peers)
    groups = min(4, heads)
    cols = heads * tok // groups
    keys = count * piece_keys
    half = tok // lax.axis_size("head")
    depth, columns = w_out.shape
    wide = 2 * columns
    vmem = pl.BlockSpec(memory_space=pltpu.VMEM)
    smem = pl.BlockSpec(memory_space=pltpu.SMEM)
    any_space = pl.BlockSpec(memory_space=pltpu.HBM)
    low_type, dma = jnp.bfloat16, pltpu.SemaphoreType.DMA
    send, lim, idx, qt = pl.pallas_call(
        functools.partial(pick_kernel, far),
        out_shape=(
            jax.ShapeDtypeStruct((far, count, 2, piece_keys, hd), cluster_kv.dtype),
            jax.ShapeDtypeStruct((2, far, count + 1), jnp.int32),
            jax.ShapeDtypeStruct((far, count + 1), jnp.int32),
            jax.ShapeDtypeStruct((groups, hd, cols), queries.dtype),
        ),
        in_specs=[smem, smem, smem, any_space, vmem],
        out_specs=(any_space, smem, smem, vmem),
        scratch_shapes=[
            pltpu.SMEM((pieces + 1,), jnp.int32),
            pltpu.VMEM((far, count, 2, piece_keys, hd), cluster_kv.dtype),
            dma((far,)),
            dma((far,)),
        ],
        name="pick",
    )(cluster_ids, piece_slot, cluster_len, cluster_kv, queries)
    return pl.pallas_call(
        functools.partial(serve_kernel, far),
        out_shape=jax.ShapeDtypeStruct((half, peers * columns), low_type),
        in_specs=[smem, smem, any_space, any_space, vmem, vmem, vmem, any_space],
        out_specs=vmem,
        scratch_shapes=[
            pltpu.VMEM((far, count, 2, piece_keys, hd), cluster_kv.dtype),
            pltpu.VMEM((far, groups, hd, cols), low_type),
            pltpu.VMEM((2, keys, hd), low_type),
            pltpu.VMEM((2, hd, keys), low_type),
            pltpu.VMEM((2, groups, 1, cols), jnp.float32),
            pltpu.VMEM((2, groups, 1, cols), jnp.float32),
            pltpu.VMEM((2, groups, hd, cols), jnp.float32),
            pltpu.VMEM((far, groups, hd, cols), low_type),
            pltpu.VMEM((far, groups, 2, cols), jnp.float32),
            pltpu.VMEM((far + 1, groups, hd, cols), low_type),
            pltpu.VMEM((far + 1, groups, 2, cols), jnp.float32),
            pltpu.VMEM((far, groups, tok, depth // groups), low_type),
            pltpu.VMEM((2, depth, columns), w_out.dtype),
            pltpu.VMEM((far, 2, half, wide), jnp.float32),
            pltpu.VMEM((far, half, wide), jnp.float32),
            pltpu.VMEM((far, half, wide), low_type),
            dma((2,)),
            dma((far,)),
            dma((far,)),
            dma((2, far, groups)),
            dma((far, groups)),
            dma((far, groups)),
            dma((far + 1, groups)),
            dma((far, groups)),
            dma((far + 1, groups)),
            dma((2, far, groups)),
            dma((far, groups)),
            dma((groups,)),
            dma((groups,)),
            dma((groups,)),
            dma((groups,)),
            dma((far,)),
            dma((far,)),
            dma((far,)),
            dma((far,)),
        ],
        compiler_params=pltpu.CompilerParams(
            collective_id=0, has_side_effects=True, vmem_limit_bytes=62 * 2**20),
        name="serve",
    )(lim, idx, send, qt, new_keys[:, 0], new_values[:, 0], cluster_kv, w_out)


def solution(mesh):
    return jax.shard_map(
        local,
        mesh=mesh,
        in_specs=(
            P(("groups", "req"), "head", None),
            P(("groups", "req"), "head", None),
            P(("groups", "req"), "head", None),
            P(("groups", "req"), "head", None, None, None),
            P("groups"),
            P("groups", None),
            P("groups", "head", None),
            P("head", "req"),
        ),
        out_specs=P(("groups", "req", "head"), None),
        check_vma=False,
    )
```

```python
import functools

import jax
import jax.numpy as jnp
from jax import lax
from jax.experimental import pallas as pl
from jax.experimental.pallas import tpu as pltpu
from jax.sharding import PartitionSpec as P

MESH = pl.DeviceIdType.MESH
NEG = -1e30
LOG2E = 1.4426950408889634


def serve_kernel(far, ids_ref, slot_ref, len_ref, q_ref, k_ref, v_ref, kv_ref, w_ref, out_ref,
                 lim_ref, idx_ref, held, gift, nbr, qt, kb, vb, top, total, acc, mine, mine_st, came, came_st, full, wv, part, got, low,
                 load_sem, kv_send, kv_recv, q_send, q_recv, p_send, p_recv, s_send, s_recv, a_send, a_recv,
                 wy_send, wy_recv, wx_send, wx_recv, part_send, part_recv, out_send, out_recv):
    me = lax.axis_index("req")
    head = lax.axis_index("head")
    grp = lax.axis_index("groups")
    hi, lo = me // 2, me % 2
    end = far - 1
    pair = {"req": me + 1 - 2 * lo}
    twin = {"groups": grp + 1 - 2 * (grp % 2)}
    mate = {"head": 1 - head}

    tok, hd = k_ref.shape
    heads = q_ref.shape[1]
    count, piece_keys = gift.shape[1], gift.shape[3]
    keys = count * piece_keys
    _, groups, _, cols = qt.shape
    sel = ids_ref.shape[0]
    pieces = slot_ref.shape[1]
    per = count // sel
    slots = held.shape[0]
    per_group = cols // tok
    block = min(128, cols)
    factor = hd ** (-0.5) * LOG2E
    half = out_ref.shape[0]
    depth, columns = w_ref.shape
    wide = 2 * columns
    slab = depth // (2 * groups)
    slice_depth = depth // groups

    def at(z):
        return {"req": z * 2 + lo}

    load_kv = pltpu.make_async_copy(kv_ref, held, load_sem.at[0])
    load_w = pltpu.make_async_copy(w_ref, wv.at[lo], load_sem.at[1])
    load_kv.start()
    load_w.start()

    barrier = pltpu.get_barrier_semaphore()
    for k in range(1, far):
        pl.semaphore_signal(barrier, inc=1, device_id=at(lax.rem(hi + k, far)), device_id_type=MESH)
    for device in (pair, twin, mate):
        pl.semaphore_signal(barrier, inc=1, device_id=device, device_id_type=MESH)

    rising = hi < end - hi
    shorter = jnp.where(rising, hi, end - hi)

    at_end = (hi == 0) | (hi == end)

    ahead = jnp.logical_not(at_end) & (end - 2 * shorter == 1)

    def order(i):
        i = jnp.where(ahead & ((i == 1) | (i == 2)), 3 - i, i)
        n = far - i
        both = n <= 2 * shorter
        d = jnp.where(both, (n + 1) // 2, n - shorter)
        above = jnp.where(both, (n % 2 == 1) == rising, rising)
        return jnp.where((i == 0) | (i == far), hi, jnp.where(above, hi + d, hi - d))

    def q_copy(z, g, to, way):
        return pltpu.make_async_remote_copy(
            src_ref=qt.at[z, g], dst_ref=qt.at[z, g], send_sem=q_send.at[way, z, g],
            recv_sem=q_recv.at[z, g], device_id=at(to), device_id_type=MESH)

    def a_copy(z, g, to, way):
        return pltpu.make_async_remote_copy(
            src_ref=full.at[z, g], dst_ref=full.at[z, g], send_sem=a_send.at[way, z, g],
            recv_sem=a_recv.at[z, g], device_id=at(to), device_id_type=MESH)

    def kv_copy(z):
        return pltpu.make_async_remote_copy(
            src_ref=gift.at[z], dst_ref=nbr.at[z], send_sem=kv_send.at[z],
            recv_sem=kv_recv.at[z], device_id=pair, device_id_type=MESH)

    def w_rows(which, c):
        return pl.ds(pl.multiple_of((which * groups + c) * slab, slab), slab)

    def wy_copy(c, slot):
        rows = w_rows(grp % 2, c)
        return pltpu.make_async_remote_copy(
            src_ref=w_ref.at[rows], dst_ref=wv.at[slot, rows], send_sem=wy_send.at[c],
            recv_sem=wy_recv.at[c], device_id=pair, device_id_type=MESH)

    def wx_copy(c, which):
        rows = w_rows(which, c)
        return pltpu.make_async_remote_copy(
            src_ref=wv.at[1 - lo, rows], dst_ref=wv.at[1 - lo, rows], send_sem=wx_send.at[c],
            recv_sem=wx_recv.at[c], device_id=twin, device_id_type=MESH)

    def inner(b):
        return jnp.where(hi > b, hi - 1, hi + 1)

    def part_pair(b, g, slot, to):
        return (
            pltpu.make_async_remote_copy(
                src_ref=mine.at[b, g], dst_ref=came.at[slot, g], send_sem=p_send.at[b, g],
                recv_sem=p_recv.at[slot, g], device_id=at(to), device_id_type=MESH),
            pltpu.make_async_remote_copy(
                src_ref=mine_st.at[b, g], dst_ref=came_st.at[slot, g], send_sem=s_send.at[b, g],
                recv_sem=s_recv.at[slot, g], device_id=at(to), device_id_type=MESH))

    def part_start(b, g):
        to = inner(b)
        slot = jnp.where((to == b) & (hi > b), far, b)
        for copy in part_pair(b, g, slot, to):
            copy.start()

    def part_wait(b, g, slot):
        for copy in part_pair(b, g, slot, jnp.where(hi < end, hi + 1, hi - 1)):
            copy.wait_recv()

    def find(c, base, also=None):
        locs, lims = [jnp.int32(0)] * per, [jnp.int32(0)] * per
        n = jnp.int32(0)
        fill = len_ref[c]
        for p in range(pieces):
            loc = slot_ref[c, p] - base
            hit = (loc >= 0) & (loc < slots)
            left = fill - p * piece_keys
            for j in range(per):
                take = hit & (n == j)
                locs[j] = jnp.where(take, loc, locs[j])
                lims[j] = jnp.where(take, left, lims[j])
            n = n + hit.astype(jnp.int32)
        return locs, lims

    def plan(z, s):
        c = ids_ref[s, z * 2 + lo]
        locs, lims = find(c, me * slots)
        _, others = find(c, (me + 1 - 2 * lo) * slots)
        for j in range(per):
            idx_ref[z, s * per + j] = locs[j]
            lim_ref[0, z, s * per + j] = lims[j]
            lim_ref[1, z, s * per + j] = others[j]

    def give(z):
        found = []
        for s in range(sel):
            found += find(ids_ref[s, z * 2 + 1 - lo], me * slots)[0]
        return found

    def wrap(z, found):
        for j in range(count):
            gift[z, j] = held[found[j], 0]
        kv_copy(z).start()

    for h in range(heads):
        at_h = h % per_group
        qt[hi, h // per_group, :, at_h * tok:(at_h + 1) * tok] = q_ref[:, h, :].T
    found = give(order(1))
    for s in range(sel):
        plan(hi, s)
        plan(order(1), s)
    pl.semaphore_wait(barrier, far + 2)

    def first(gap):
        return jnp.where((gap == 0) | (3 * gap >= 2 * groups), groups, (3 * gap + 1) // 2)

    def intake(n, g, upper):
        above, below = end - n + 1, n - 1

        @pl.when(upper & (above > hi))
        def _():
            q_copy(above, g, hi, 1).wait_recv()

            @pl.when(hi > 0)
            def _():
                q_copy(above, g, hi - 1, 1).start()

        @pl.when(jnp.logical_not(upper) & (below < hi))
        def _():
            q_copy(below, g, hi, 0).wait_recv()

            @pl.when(hi < end)
            def _():
                q_copy(below, g, hi + 1, 0).start()

    @pl.loop(0, groups)
    def _(g):
        @pl.when((hi < end) & (g < first(hi)))
        def _():
            q_copy(hi, g, hi + 1, 0).start()

        @pl.when((hi > 0) & (g < first(end - hi)))
        def _():
            q_copy(hi, g, hi - 1, 1).start()

    load_kv.wait()
    wrap(order(1), found)

    @pl.loop(2, far + 1)
    def _(i):
        z = order(i)
        wrap(z, give(z))

    @pl.loop(0, groups)
    def _(c):
        wy_copy(c, lo).start()

    own_vt = v_ref[...].T
    own_k = k_ref[...]

    @pl.loop(0, groups)
    def _(g):
        s = jnp.dot(own_k, qt[hi, g], preferred_element_type=jnp.float32)
        u = lax.broadcasted_iota(jnp.int32, s.shape, 0)
        t = lax.broadcasted_iota(jnp.int32, s.shape, 1) % tok
        s = jnp.where(u <= t, s, NEG)
        m = jnp.max(s, axis=0, keepdims=True)
        w = jnp.exp2((s - m) * factor)
        top[0, g] = m
        total[0, g] = jnp.sum(w, axis=0, keepdims=True)
        acc[0, g] = jnp.dot(own_vt, w.astype(jnp.bfloat16), preferred_element_type=jnp.float32)

    def unit(z, side, src, slot, g):
        fills = [lim_ref[side, z, i] for i in range(count)]
        key = lax.broadcasted_iota(jnp.int32, (piece_keys, block), 0)

        def score(b):
            s = jnp.dot(kb[src], qt[z, g, :, b * block:(b + 1) * block], preferred_element_type=jnp.float32)
            return jnp.concatenate(
                [jnp.where(key < fills[i], s[i * piece_keys:(i + 1) * piece_keys], NEG) for i in range(count)], axis=0)

        def weigh(b, s):
            at_b = slice(b * block, (b + 1) * block)
            m_old = top[slot, g, :, at_b]
            m = jnp.maximum(m_old, jnp.max(s, axis=0, keepdims=True))
            keep = jnp.exp2((m_old - m) * factor)
            w = jnp.exp2((s - m) * factor)
            mixed = jnp.dot(vb[src], w.astype(jnp.bfloat16), preferred_element_type=jnp.float32)
            top[slot, g, :, at_b] = m
            total[slot, g, :, at_b] = total[slot, g, :, at_b] * keep + jnp.sum(w, axis=0, keepdims=True)
            acc[slot, g, :, at_b] = acc[slot, g, :, at_b] * keep + mixed

        s = score(0)
        for b in range(cols // block):
            ahead = score(b + 1) if b + 1 < cols // block else None
            weigh(b, s)
            s = ahead

    def blend(m1, l1, a1, m2, l2, a2):
        m = jnp.maximum(m1, m2)
        f1 = jnp.exp2((m1 - m) * factor)
        f2 = jnp.exp2((m2 - m) * factor)
        return m, l1 * f1 + l2 * f2, a1 * f1 + a2 * f2

    def merge(b, g):
        part_wait(b, g, b)
        m, l, a = blend(
            mine_st[b, g, 0:1], mine_st[b, g, 1:2], mine[b, g].astype(jnp.float32),
            came_st[b, g, 0:1], came_st[b, g, 1:2], came[b, g].astype(jnp.float32))
        mine_st[b, g, 0:1] = m
        mine_st[b, g, 1:2] = l
        mine[b, g] = a.astype(jnp.bfloat16)
        part_start(b, g)

    def absorb(slot, g):
        part_wait(hi, g, slot)
        m, l, a = blend(
            top[0, g], total[0, g], acc[0, g],
            came_st[slot, g, 0:1], came_st[slot, g, 1:2], came[slot, g].astype(jnp.float32))
        top[0, g] = m
        total[0, g] = l
        acc[0, g] = a

    def stage(z, buf):
        for j in range(count):
            at_j = slice(j * piece_keys, (j + 1) * piece_keys)
            loc = idx_ref[z, j]
            kb[buf, at_j] = held[loc, 0, 0]
            vb[buf, :, at_j] = held[loc, 0, 1].T

    @pl.loop(0, far + 1)
    def _(i):
        b = order(i)
        slot = jnp.where(b == hi, 0, 1)
        closing = i == far
        middle = (i > 0) & (i < far)

        @pl.when(i < far)
        def _():
            stage(b, 0)

        @pl.when((ahead & (i == 0)) | (jnp.logical_not(ahead) & middle) | (middle & (i > 1)))
        def _():
            top[1] = jnp.full_like(top[1], NEG)
            total[1] = jnp.zeros_like(total[1])
            acc[1] = jnp.zeros_like(acc[1])

        @pl.when(ahead & (i == 0))
        def _():
            stage(order(1), 1)

        @pl.when(i > 0)
        def _():
            kv_copy(b).wait_recv()
            for j in range(count):
                at_j = slice(j * piece_keys, (j + 1) * piece_keys)
                kb[1, at_j] = nbr[b, j, 0]
                vb[1, :, at_j] = nbr[b, j, 1].T

        @pl.loop(0, groups)
        def _(g):
            @pl.when(at_end & middle)
            def _():
                intake(i, g, hi == 0)

            @pl.when((i < far) & jnp.logical_not(ahead & (i == 1)))
            def _():
                unit(b, 0, 0, slot, g)

            @pl.when(ahead & (i == 0))
            def _():
                intake(1, g, jnp.logical_not(rising))
                unit(order(1), 0, 1, 1, g)

            @pl.when(i > 0)
            def _():
                unit(b, 1, 1, slot, g)

            @pl.when(middle)
            def _():
                mine_st[b, g, 0:1] = top[1, g]
                mine_st[b, g, 1:2] = total[1, g]
                mine[b, g] = acc[1, g].astype(jnp.bfloat16)

                @pl.when(at_end)
                def _():
                    part_start(b, g)

            low_b = i - 1 - end + hi
            high_b = far + hi - i

            @pl.when((low_b >= 0) & (low_b < hi) & (hi < end))
            def _():
                merge(low_b, g)

            @pl.when((high_b > hi) & (high_b <= end) & (hi > 0))
            def _():
                merge(high_b, g)

            @pl.when(closing)
            def _():
                @pl.when(hi > 0)
                def _():
                    absorb(hi, g)

                @pl.when(hi < end)
                def _():
                    absorb(far, g)

                o = acc[0, g] / total[0, g]
                for h in range(per_group):
                    full[hi, g, :, h * hd:(h + 1) * hd] = o[:, h * tok:(h + 1) * tok].T.astype(full.dtype)

                @pl.when(hi < end)
                def _():
                    a_copy(hi, g, hi + 1, 0).start()

                @pl.when(hi > 0)
                def _():
                    a_copy(hi, g, hi - 1, 1).start()

            @pl.when(jnp.logical_not(at_end) & (i < end))
            def _():
                @pl.when(jnp.logical_not(ahead & (i == 0)))
                def _():
                    intake(i + 1, g, jnp.logical_not(rising))

                @pl.when(g > 0)
                def _():
                    intake(i + 1, g - 1, rising)

        @pl.when(i == 0)
        def _():
            @pl.loop(2, far)
            def _(k):
                for s in range(sel):
                    plan(order(k), s)

        @pl.when(jnp.logical_not(at_end))
        def _():
            @pl.when(i < end)
            def _():
                intake(i + 1, groups - 1, rising)

            @pl.loop(0, groups)
            def _(g):
                @pl.when((i == hi - 1) & (g >= first(hi)))
                def _():
                    q_copy(hi, g, hi + 1, 0).start()

                @pl.when((i == end - hi - 1) & (g >= first(end - hi)))
                def _():
                    q_copy(hi, g, hi - 1, 1).start()

    def part_copy(z):
        return pltpu.make_async_remote_copy(
            src_ref=part.at[z, 1 - head], dst_ref=got.at[z], send_sem=part_send.at[z],
            recv_sem=part_recv.at[z], device_id=mate, device_id_type=MESH)

    def out_copy(z, owner):
        return pltpu.make_async_remote_copy(
            src_ref=low.at[z], dst_ref=out_ref.at[:, pl.ds(pl.multiple_of(owner * wide, wide), wide)],
            send_sem=out_send.at[z], recv_sem=out_recv.at[owner], device_id=at(z), device_id_type=MESH)

    keep_copy = pltpu.make_async_copy(
        low.at[hi], out_ref.at[:, pl.ds(pl.multiple_of(hi * wide, wide), wide)], load_sem.at[2])

    def compute(z, j):
        at_j = pl.ds(pl.multiple_of(j * columns, columns), columns)
        terms = jnp.dot(full[z, 0], wv[j, 0:slice_depth], preferred_element_type=jnp.float32)
        for g in range(1, groups):
            terms += jnp.dot(full[z, g], wv[j, g * slice_depth:(g + 1) * slice_depth],
                             preferred_element_type=jnp.float32)
        part[z, 0, :, at_j] = terms[:half]
        part[z, 1, :, at_j] = terms[half:]

    def finish(z):
        part_copy(z).wait_recv()
        rows = (part[z, head] + got[z]).astype(out_ref.dtype)

        low[z] = rows

        @pl.when(z == hi)
        def _():
            keep_copy.start()

        @pl.when(z != hi)
        def _():
            out_copy(z, hi).start()

    load_w.wait()
    settle = min(2, end)

    @pl.loop(0, far)
    def _(d):
        @pl.when(d > 0)
        def _():
            @pl.loop(0, groups)
            def _(g):
                @pl.loop(0, 2)
                def _(turn):
                    above = (turn == 0) == rising

                    @pl.when(jnp.logical_not(above) & (hi - d >= 0))
                    def _():
                        a_copy(hi - d, g, hi, 0).wait_recv()

                        @pl.when(hi < end)
                        def _():
                            a_copy(hi - d, g, hi + 1, 0).start()

                    @pl.when(above & (hi + d <= end))
                    def _():
                        a_copy(hi + d, g, hi, 1).wait_recv()

                        @pl.when(hi > 0)
                        def _():
                            a_copy(hi + d, g, hi - 1, 1).start()

                @pl.when(d == 1)
                def _():
                    wy_copy(g, 1 - lo).wait_recv()
                    wx_copy(g, grp % 2).start()

        @pl.when(d == settle)
        def _():
            @pl.loop(0, groups)
            def _(c):
                wx_copy(c, 1 - grp % 2).wait_recv()

            @pl.loop(0, 2 * settle - 1)
            def _(n):
                z = hi - (settle - 1) + n

                @pl.when((z >= 0) & (z < far))
                def _():
                    compute(z, 1 - lo)
                    part_copy(z).start()

        @pl.loop(0, 2)
        def _(side):
            z = hi + d * (2 * side - 1)

            @pl.when((z >= 0) & (z < far) & ((d > 0) | (side == 0)))
            def _():
                compute(z, lo)

                @pl.when(d >= settle)
                def _():
                    compute(z, 1 - lo)
                    part_copy(z).start()

    @pl.loop(0, far)
    def _(d):
        @pl.loop(0, 2)
        def _(side):
            z = hi + d * (2 * side - 1)

            @pl.when((z >= 0) & (z < far) & ((d > 0) | (side == 0)))
            def _():
                finish(z)

    @pl.loop(0, groups)
    def _(g):
        wy_copy(g, lo).wait_send()
        wx_copy(g, grp % 2).wait_send()

    @pl.loop(0, far)
    def _(z):
        kv_copy(z).wait_send()
        part_copy(z).wait_send()

        @pl.loop(0, groups)
        def _(g):
            @pl.when((z <= hi) & (hi < end))
            def _():
                q_copy(z, g, hi + 1, 0).wait_send()
                a_copy(z, g, hi + 1, 0).wait_send()

            @pl.when((z >= hi) & (hi > 0))
            def _():
                q_copy(z, g, hi - 1, 1).wait_send()
                a_copy(z, g, hi - 1, 1).wait_send()

            @pl.when(z != hi)
            def _():
                for copy in part_pair(z, g, z, inner(z)):
                    copy.wait_send()

        @pl.when(z != hi)
        def _():
            out_copy(z, hi).wait_send()
            out_copy(z, z).wait_recv()

    keep_copy.wait()


def local(queries, new_keys, new_values, cluster_kv, cluster_len, piece_slot, cluster_ids, w_out):
    peers = lax.axis_size("req")
    far = peers // 2
    tok, heads, hd = queries.shape
    piece_keys = cluster_kv.shape[3]
    pieces = piece_slot.shape[1]
    sel = cluster_ids.shape[2]
    count = sel * (pieces // peers)
    groups = min(4, heads)
    cols = heads * tok // groups
    keys = count * piece_keys
    half = tok // lax.axis_size("head")
    depth, columns = w_out.shape
    wide = 2 * columns
    vmem = pl.BlockSpec(memory_space=pltpu.VMEM)
    smem = pl.BlockSpec(memory_space=pltpu.SMEM)
    any_space = pl.BlockSpec(memory_space=pltpu.HBM)
    low_type, dma = jnp.bfloat16, pltpu.SemaphoreType.DMA
    return pl.pallas_call(
        functools.partial(serve_kernel, far),
        out_shape=jax.ShapeDtypeStruct((half, peers * columns), low_type),
        in_specs=[smem, smem, smem, vmem, vmem, vmem, any_space, any_space],
        out_specs=any_space,
        scratch_shapes=[
            pltpu.SMEM((2, far, count), jnp.int32),
            pltpu.SMEM((far, count), jnp.int32),
            pltpu.VMEM(cluster_kv.shape, cluster_kv.dtype),
            pltpu.VMEM((far, count, 2, piece_keys, hd), cluster_kv.dtype),
            pltpu.VMEM((far, count, 2, piece_keys, hd), cluster_kv.dtype),
            pltpu.VMEM((far, groups, hd, cols), low_type),
            pltpu.VMEM((2, keys, hd), low_type),
            pltpu.VMEM((2, hd, keys), low_type),
            pltpu.VMEM((2, groups, 1, cols), jnp.float32),
            pltpu.VMEM((2, groups, 1, cols), jnp.float32),
            pltpu.VMEM((2, groups, hd, cols), jnp.float32),
            pltpu.VMEM((far, groups, hd, cols), low_type),
            pltpu.VMEM((far, groups, 2, cols), jnp.float32),
            pltpu.VMEM((far + 1, groups, hd, cols), low_type),
            pltpu.VMEM((far + 1, groups, 2, cols), jnp.float32),
            pltpu.VMEM((far, groups, tok, depth // groups), low_type),
            pltpu.VMEM((2, depth, columns), w_out.dtype),
            pltpu.VMEM((far, 2, half, wide), jnp.float32),
            pltpu.VMEM((far, half, wide), jnp.float32),
            pltpu.VMEM((far, half, wide), low_type),
            dma((3,)),
            dma((far,)),
            dma((far,)),
            dma((2, far, groups)),
            dma((far, groups)),
            dma((far, groups)),
            dma((far + 1, groups)),
            dma((far, groups)),
            dma((far + 1, groups)),
            dma((2, far, groups)),
            dma((far, groups)),
            dma((groups,)),
            dma((groups,)),
            dma((groups,)),
            dma((groups,)),
            dma((far,)),
            dma((far,)),
            dma((far,)),
            dma((far,)),
        ],
        compiler_params=pltpu.CompilerParams(
            collective_id=0, has_side_effects=True, vmem_limit_bytes=62 * 2**20),
        name="serve",
    )(cluster_ids[:, 0].T, piece_slot, cluster_len, queries, new_keys[:, 0], new_values[:, 0], cluster_kv, w_out)


def solution(mesh):
    return jax.shard_map(
        local,
        mesh=mesh,
        in_specs=(
            P(("groups", "req"), "head", None),
            P(("groups", "req"), "head", None),
            P(("groups", "req"), "head", None),
            P(("groups", "req"), "head", None, None, None),
            P("groups"),
            P("groups", None),
            P("groups", "head", None),
            P("head", "req"),
        ),
        out_specs=P(("groups", "req", "head"), None),
        check_vma=False,
    )
```

```python
import functools

import jax
import jax.numpy as jnp
from jax import lax
from jax.experimental import pallas as pl
from jax.experimental.pallas import tpu as pltpu
from jax.sharding import PartitionSpec as P

MESH = pl.DeviceIdType.MESH
NEG = -1e30
LOG2E = 1.4426950408889634


def serve_kernel(far, ids_ref, slot_ref, len_ref, q_ref, k_ref, v_ref, kv_ref, w_ref, out_ref,
                 lim_ref, idx_ref, held, gift, vt, nbr, qt, kb, vb, top, total, acc, mine, mine_st, came, came_st, full, wv, part, got, low,
                 load_sem, kv_send, kv_recv, q_send, q_recv, p_send, p_recv, s_send, s_recv, a_send, a_recv,
                 wy_send, wy_recv, wx_send, wx_recv, part_send, part_recv, out_send, out_recv):
    me = lax.axis_index("req")
    head = lax.axis_index("head")
    grp = lax.axis_index("groups")
    hi, lo = me // 2, me % 2
    end = far - 1
    pair = {"req": me + 1 - 2 * lo}
    twin = {"groups": grp + 1 - 2 * (grp % 2)}
    mate = {"head": 1 - head}

    tok, hd = k_ref.shape
    heads = q_ref.shape[1]
    count, piece_keys = gift.shape[1], gift.shape[3]
    keys = count * piece_keys
    _, groups, _, cols = qt.shape
    sel = ids_ref.shape[0]
    pieces = slot_ref.shape[1]
    per = count // sel
    slots = held.shape[0]
    per_group = cols // tok
    block = min(256, cols)
    factor = hd ** (-0.5) * LOG2E
    half = out_ref.shape[0]
    depth, columns = w_ref.shape
    wide = 2 * columns
    slab = depth // (2 * groups)
    slice_depth = depth // groups

    def at(z):
        return {"req": z * 2 + lo}

    load_kv = pltpu.make_async_copy(kv_ref, held, load_sem.at[0])
    load_w = pltpu.make_async_copy(w_ref, wv.at[lo], load_sem.at[1])
    load_kv.start()
    load_w.start()

    barrier = pltpu.get_barrier_semaphore()
    for k in range(1, far):
        pl.semaphore_signal(barrier, inc=1, device_id=at(lax.rem(hi + k, far)), device_id_type=MESH)
    for device in (pair, twin, mate):
        pl.semaphore_signal(barrier, inc=1, device_id=device, device_id_type=MESH)

    rising = hi < end - hi
    shorter = jnp.where(rising, hi, end - hi)

    at_end = (hi == 0) | (hi == end)

    ahead = jnp.logical_not(at_end) & (end - 2 * shorter == 1)

    def order(i):
        i = jnp.where(ahead & ((i == 1) | (i == 2)), 3 - i, i)
        n = far - i
        both = n <= 2 * shorter
        d = jnp.where(both, (n + 1) // 2, n - shorter)
        above = jnp.where(both, (n % 2 == 1) == rising, rising)
        return jnp.where((i == 0) | (i == far), hi, jnp.where(above, hi + d, hi - d))

    def q_copy(z, g, to, way):
        return pltpu.make_async_remote_copy(
            src_ref=qt.at[z, g], dst_ref=qt.at[z, g], send_sem=q_send.at[way, z],
            recv_sem=q_recv.at[z, g], device_id=at(to), device_id_type=MESH)

    def a_copy(z, g, to, way):
        return pltpu.make_async_remote_copy(
            src_ref=full.at[z, g], dst_ref=full.at[z, g], send_sem=a_send.at[way, z],
            recv_sem=a_recv.at[z, g], device_id=at(to), device_id_type=MESH)

    def kv_copy(z):
        return pltpu.make_async_remote_copy(
            src_ref=gift.at[z], dst_ref=nbr.at[z], send_sem=kv_send,
            recv_sem=kv_recv.at[z], device_id=pair, device_id_type=MESH)

    def w_rows(which, c):
        return pl.ds(pl.multiple_of((which * groups + c) * slab, slab), slab)

    def wy_copy(c, slot):
        rows = w_rows(grp % 2, c)
        return pltpu.make_async_remote_copy(
            src_ref=w_ref.at[rows], dst_ref=wv.at[slot, rows], send_sem=wy_send,
            recv_sem=wy_recv.at[c], device_id=pair, device_id_type=MESH)

    def wx_copy(c, which):
        rows = w_rows(which, c)
        return pltpu.make_async_remote_copy(
            src_ref=wv.at[1 - lo, rows], dst_ref=wv.at[1 - lo, rows], send_sem=wx_send,
            recv_sem=wx_recv.at[c], device_id=twin, device_id_type=MESH)

    def pass_w(c):
        wy_copy(c, 1 - lo).wait_recv()
        wx_copy(c, grp % 2).start()

    def inner(b):
        return jnp.where(hi > b, hi - 1, hi + 1)

    def part_pair(b, g, slot, to):
        return (
            pltpu.make_async_remote_copy(
                src_ref=mine.at[b, g], dst_ref=came.at[slot, g], send_sem=p_send.at[b],
                recv_sem=p_recv.at[slot, g], device_id=at(to), device_id_type=MESH),
            pltpu.make_async_remote_copy(
                src_ref=mine_st.at[b, g], dst_ref=came_st.at[slot, g], send_sem=s_send.at[b],
                recv_sem=s_recv.at[slot, g], device_id=at(to), device_id_type=MESH))

    def part_start(b, g):
        to = inner(b)
        slot = jnp.where((to == b) & (hi > b), far, b)
        for copy in part_pair(b, g, slot, to):
            copy.start()

    def part_wait(b, g, slot):
        for copy in part_pair(b, g, slot, jnp.where(hi < end, hi + 1, hi - 1)):
            copy.wait_recv()

    def find(c, base, also=None):
        locs, lims = [jnp.int32(0)] * per, [jnp.int32(0)] * per
        n = jnp.int32(0)
        fill = len_ref[c]
        for p in range(pieces):
            loc = slot_ref[c, p] - base
            hit = (loc >= 0) & (loc < slots)
            left = fill - p * piece_keys
            for j in range(per):
                take = hit & (n == j)
                locs[j] = jnp.where(take, loc, locs[j])
                lims[j] = jnp.where(take, left, lims[j])
            n = n + hit.astype(jnp.int32)
        return locs, lims

    def plan(z, s):
        c = ids_ref[s, z * 2 + lo]
        locs, lims = find(c, me * slots)
        _, others = find(c, (me + 1 - 2 * lo) * slots)
        for j in range(per):
            idx_ref[z, s * per + j] = locs[j]
            lim_ref[0, z, s * per + j] = lims[j]
            lim_ref[1, z, s * per + j] = others[j]

    def give(z):
        found = []
        for s in range(sel):
            found += find(ids_ref[s, z * 2 + 1 - lo], me * slots)[0]
        return found

    def wrap(z, found):
        for j in range(count):
            gift[z, j] = held[found[j], 0]
        kv_copy(z).start()

    for h in range(heads):
        at_h = h % per_group
        qt[hi, h // per_group, :, at_h * tok:(at_h + 1) * tok] = q_ref[:, h, :].T
    vt[...] = v_ref[...].T
    found = give(order(1))
    for s in range(sel):
        plan(hi, s)
        plan(order(1), s)
    pl.semaphore_wait(barrier, far + 2)

    def first(gap):
        return jnp.where((gap == 0) | (3 * gap >= 2 * groups), groups, (3 * gap + 1) // 2)

    def intake(n, g, upper):
        above, below = end - n + 1, n - 1

        @pl.when(upper & (above > hi))
        def _():
            q_copy(above, g, hi, 1).wait_recv()

            @pl.when(hi > 0)
            def _():
                q_copy(above, g, hi - 1, 1).start()

        @pl.when(jnp.logical_not(upper) & (below < hi))
        def _():
            q_copy(below, g, hi, 0).wait_recv()

            @pl.when(hi < end)
            def _():
                q_copy(below, g, hi + 1, 0).start()

    @pl.loop(0, groups)
    def _(g):
        @pl.when((hi < end) & (g < first(hi)))
        def _():
            q_copy(hi, g, hi + 1, 0).start()

        @pl.when((hi > 0) & (g < first(end - hi)))
        def _():
            q_copy(hi, g, hi - 1, 1).start()

    load_kv.wait()
    wrap(order(1), found)

    @pl.loop(2, far + 1)
    def _(i):
        z = order(i)
        wrap(z, give(z))

    @pl.loop(0, groups)
    def _(c):
        wy_copy(c, lo).start()

    def begin(g):
        s = jnp.dot(k_ref[...], qt[hi, g], preferred_element_type=jnp.float32)
        u = lax.broadcasted_iota(jnp.int32, s.shape, 0)
        t = lax.broadcasted_iota(jnp.int32, s.shape, 1) % tok
        s = jnp.where(u <= t, s, NEG)
        m = jnp.max(s, axis=0, keepdims=True)
        w = jnp.exp2((s - m) * factor)
        top[0, g] = m
        total[0, g] = jnp.sum(w, axis=0, keepdims=True)
        acc[0, g] = jnp.dot(vt[...], w.astype(jnp.bfloat16), preferred_element_type=jnp.float32)

    def unit(z, parts, slot, g):
        key = lax.broadcasted_iota(jnp.int32, (piece_keys, block), 0)
        steps = [(side, src, b) for side, src in parts for b in range(cols // block)]

        def score(side, src, b):
            s = jnp.dot(kb[src], qt[z, g, :, b * block:(b + 1) * block], preferred_element_type=jnp.float32)
            return jnp.concatenate(
                [jnp.where(key < lim_ref[side, z, i], s[i * piece_keys:(i + 1) * piece_keys], NEG)
                 for i in range(count)], axis=0)

        def weigh(src, b, s):
            at_b = slice(b * block, (b + 1) * block)
            m_old = top[slot, g, :, at_b]
            m = jnp.maximum(m_old, jnp.max(s, axis=0, keepdims=True))
            keep = jnp.exp2((m_old - m) * factor)
            w = jnp.exp2((s - m) * factor)
            mixed = jnp.dot(vb[src], w.astype(jnp.bfloat16), preferred_element_type=jnp.float32)
            top[slot, g, :, at_b] = m
            total[slot, g, :, at_b] = total[slot, g, :, at_b] * keep + jnp.sum(w, axis=0, keepdims=True)
            acc[slot, g, :, at_b] = acc[slot, g, :, at_b] * keep + mixed

        s = score(*steps[0])
        for n, (_, src, b) in enumerate(steps):
            later = score(*steps[n + 1]) if n + 1 < len(steps) else None
            weigh(src, b, s)
            s = later

    def blend(m1, l1, a1, m2, l2, a2):
        m = jnp.maximum(m1, m2)
        f1 = jnp.exp2((m1 - m) * factor)
        f2 = jnp.exp2((m2 - m) * factor)
        return m, l1 * f1 + l2 * f2, a1 * f1 + a2 * f2

    def merge(b, g):
        part_wait(b, g, b)
        m, l, a = blend(
            mine_st[b, g, 0:1], mine_st[b, g, 1:2], mine[b, g].astype(jnp.float32),
            came_st[b, g, 0:1], came_st[b, g, 1:2], came[b, g].astype(jnp.float32))
        mine_st[b, g, 0:1] = m
        mine_st[b, g, 1:2] = l
        mine[b, g] = a.astype(jnp.bfloat16)
        part_start(b, g)

    def absorb(slot, g):
        part_wait(hi, g, slot)
        m, l, a = blend(
            top[0, g], total[0, g], acc[0, g],
            came_st[slot, g, 0:1], came_st[slot, g, 1:2], came[slot, g].astype(jnp.float32))
        top[0, g] = m
        total[0, g] = l
        acc[0, g] = a

    def stage(z, buf):
        for j in range(count):
            at_j = slice(j * piece_keys, (j + 1) * piece_keys)
            loc = idx_ref[z, j]
            kb[buf, at_j] = held[loc, 0, 0]
            vb[buf, :, at_j] = held[loc, 0, 1].T

    @pl.loop(0, far + 1)
    def _(i):
        b = order(i)
        slot = jnp.where(b == hi, 0, 1)
        closing = i == far
        middle = (i > 0) & (i < far)

        @pl.when(i < far)
        def _():
            stage(b, 0)

        @pl.when((ahead & (i == 0)) | (jnp.logical_not(ahead) & middle) | (middle & (i > 1)))
        def _():
            top[1] = jnp.full_like(top[1], NEG)
            total[1] = jnp.zeros_like(total[1])
            acc[1] = jnp.zeros_like(acc[1])

        @pl.when(ahead & (i == 0))
        def _():
            stage(order(1), 1)

        @pl.when(i > 0)
        def _():
            kv_copy(b).wait_recv()
            for j in range(count):
                at_j = slice(j * piece_keys, (j + 1) * piece_keys)
                kb[1, at_j] = nbr[b, j, 0]
                vb[1, :, at_j] = nbr[b, j, 1].T

        @pl.loop(0, groups)
        def _(g):
            @pl.when(at_end & middle)
            def _():
                intake(i, g, hi == 0)

            alone = (i == far) | (ahead & (i == 1))

            @pl.when(i == 0)
            def _():
                begin(g)
                unit(b, [(0, 0)], slot, g)

            @pl.when(ahead & (i == 0))
            def _():
                intake(1, g, jnp.logical_not(rising))
                unit(order(1), [(0, 1)], 1, g)

            @pl.when(alone)
            def _():
                unit(b, [(1, 1)], slot, g)

            @pl.when((i > 0) & jnp.logical_not(alone))
            def _():
                unit(b, [(0, 0), (1, 1)], slot, g)

            @pl.when(middle)
            def _():
                mine_st[b, g, 0:1] = top[1, g]
                mine_st[b, g, 1:2] = total[1, g]
                mine[b, g] = acc[1, g].astype(jnp.bfloat16)

                @pl.when(at_end)
                def _():
                    part_start(b, g)

            low_b = i - 1 - end + hi
            high_b = far + hi - i

            @pl.when((low_b >= 0) & (low_b < hi) & (hi < end))
            def _():
                merge(low_b, g)

            @pl.when((high_b > hi) & (high_b <= end) & (hi > 0))
            def _():
                merge(high_b, g)

            @pl.when(closing)
            def _():
                @pl.when(hi > 0)
                def _():
                    absorb(hi, g)

                @pl.when(hi < end)
                def _():
                    absorb(far, g)

                o = acc[0, g] / total[0, g]
                for h in range(per_group):
                    full[hi, g, :, h * hd:(h + 1) * hd] = o[:, h * tok:(h + 1) * tok].T.astype(full.dtype)

                @pl.when(hi < end)
                def _():
                    a_copy(hi, g, hi + 1, 0).start()

                @pl.when(hi > 0)
                def _():
                    a_copy(hi, g, hi - 1, 1).start()

                @pl.when(g == groups - 1)
                def _():
                    pass_w(0)

            @pl.when(jnp.logical_not(at_end))
            def _():
                @pl.when((i < end) & jnp.logical_not(ahead & (i == 0)))
                def _():
                    intake(i + 1, g, jnp.logical_not(rising))

                @pl.when((i < end) & (g > 0))
                def _():
                    intake(i + 1, g - 1, rising)

                @pl.when((i > 0) & (i <= end) & (g == 0))
                def _():
                    intake(i, groups - 1, rising)

        @pl.when(i == 0)
        def _():
            @pl.loop(2, far)
            def _(k):
                for s in range(sel):
                    plan(order(k), s)

        @pl.when(jnp.logical_not(at_end))
        def _():
            @pl.loop(0, groups)
            def _(g):
                @pl.when((i == hi - 1) & (g >= first(hi)))
                def _():
                    q_copy(hi, g, hi + 1, 0).start()

                @pl.when((i == end - hi - 1) & (g >= first(end - hi)))
                def _():
                    q_copy(hi, g, hi - 1, 1).start()

    def part_copy(z):
        return pltpu.make_async_remote_copy(
            src_ref=part.at[z, 1 - head], dst_ref=got.at[z], send_sem=part_send,
            recv_sem=part_recv.at[z], device_id=mate, device_id_type=MESH)

    def out_copy(z, owner):
        return pltpu.make_async_remote_copy(
            src_ref=low.at[z], dst_ref=out_ref.at[:, pl.ds(pl.multiple_of(owner * wide, wide), wide)],
            send_sem=out_send, recv_sem=out_recv.at[owner], device_id=at(z), device_id_type=MESH)

    keep_copy = pltpu.make_async_copy(
        low.at[hi], out_ref.at[:, pl.ds(pl.multiple_of(hi * wide, wide), wide)], load_sem.at[2])

    def compute(z, j):
        at_j = pl.ds(pl.multiple_of(j * columns, columns), columns)
        terms = jnp.dot(full[z, 0], wv[j, 0:slice_depth], preferred_element_type=jnp.float32)
        for g in range(1, groups):
            terms += jnp.dot(full[z, g], wv[j, g * slice_depth:(g + 1) * slice_depth],
                             preferred_element_type=jnp.float32)
        part[z, 0, :, at_j] = terms[:half]
        part[z, 1, :, at_j] = terms[half:]

    def finish(z):
        part_copy(z).wait_recv()
        rows = (part[z, head] + got[z]).astype(out_ref.dtype)

        low[z] = rows

        @pl.when(z == hi)
        def _():
            keep_copy.start()

        @pl.when(z != hi)
        def _():
            out_copy(z, hi).start()

    load_w.wait()
    settle = min(2, end)

    @pl.loop(0, far)
    def _(d):
        @pl.when(d > 0)
        def _():
            @pl.loop(0, groups)
            def _(g):
                @pl.loop(0, 2)
                def _(turn):
                    above = (turn == 0) == rising

                    @pl.when(jnp.logical_not(above) & (hi - d >= 0))
                    def _():
                        a_copy(hi - d, g, hi, 0).wait_recv()

                        @pl.when(hi < end)
                        def _():
                            a_copy(hi - d, g, hi + 1, 0).start()

                    @pl.when(above & (hi + d <= end))
                    def _():
                        a_copy(hi + d, g, hi, 1).wait_recv()

                        @pl.when(hi > 0)
                        def _():
                            a_copy(hi + d, g, hi - 1, 1).start()

                @pl.when((d == 1) & (g < groups - 1))
                def _():
                    pass_w(g + 1)

        def around(reach, act):
            @pl.loop(0, 2)
            def _(side):
                z = hi + reach * (2 * side - 1)

                @pl.when((z >= 0) & (z < far) & ((reach > 0) | (side == 0)))
                def _():
                    act(z)

        def within(act):
            @pl.loop(0, 2 * settle - 1)
            def _(n):
                z = hi - (settle - 1) + n

                @pl.when((z >= 0) & (z < far))
                def _():
                    act(z)

        def rest(z):
            compute(z, 1 - lo)
            part_copy(z).start()

        @pl.when(d == settle)
        def _():
            @pl.loop(0, groups)
            def _(c):
                wx_copy(c, 1 - grp % 2).wait_recv()

            within(rest)

        def whole(z):
            compute(z, lo)

            @pl.when(d >= settle)
            def _():
                rest(z)

        around(d, whole)

        @pl.when(d == settle)
        def _():
            within(finish)

        @pl.when(d > settle)
        def _():
            around(d - 1, finish)

        @pl.when(d == end)
        def _():
            around(d, finish)

    def sent(src, sem):
        pltpu.make_async_remote_copy(
            src_ref=src, dst_ref=src, send_sem=sem, recv_sem=load_sem.at[0],
            device_id=mate, device_id_type=MESH).wait_send()

    sent(w_ref.at[pl.ds(0, groups * slab)], wy_send)
    sent(w_ref.at[pl.ds(0, groups * slab)], wx_send)
    sent(gift, kv_send)
    sent(got, part_send)
    sent(low.at[pl.ds(0, end)], out_send)

    @pl.loop(0, far)
    def _(z):
        @pl.when((z <= hi) & (hi < end))
        def _():
            sent(qt.at[z], q_send.at[0, z])
            sent(full.at[z], a_send.at[0, z])

        @pl.when((z >= hi) & (hi > 0))
        def _():
            sent(qt.at[z], q_send.at[1, z])
            sent(full.at[z], a_send.at[1, z])

        @pl.when(z != hi)
        def _():
            sent(mine.at[z], p_send.at[z])
            sent(mine_st.at[z], s_send.at[z])
            out_copy(z, z).wait_recv()

    keep_copy.wait()


def local(queries, new_keys, new_values, cluster_kv, cluster_len, piece_slot, cluster_ids, w_out):
    peers = lax.axis_size("req")
    far = peers // 2
    tok, heads, hd = queries.shape
    piece_keys = cluster_kv.shape[3]
    pieces = piece_slot.shape[1]
    sel = cluster_ids.shape[2]
    count = sel * (pieces // peers)
    groups = min(4, heads)
    cols = heads * tok // groups
    keys = count * piece_keys
    half = tok // lax.axis_size("head")
    depth, columns = w_out.shape
    wide = 2 * columns
    vmem = pl.BlockSpec(memory_space=pltpu.VMEM)
    smem = pl.BlockSpec(memory_space=pltpu.SMEM)
    any_space = pl.BlockSpec(memory_space=pltpu.HBM)
    low_type, dma = jnp.bfloat16, pltpu.SemaphoreType.DMA
    return pl.pallas_call(
        functools.partial(serve_kernel, far),
        out_shape=jax.ShapeDtypeStruct((half, peers * columns), low_type),
        in_specs=[smem, smem, smem, vmem, vmem, vmem, any_space, any_space],
        out_specs=any_space,
        scratch_shapes=[
            pltpu.SMEM((2, far, count), jnp.int32),
            pltpu.SMEM((far, count), jnp.int32),
            pltpu.VMEM(cluster_kv.shape, cluster_kv.dtype),
            pltpu.VMEM((far, count, 2, piece_keys, hd), cluster_kv.dtype),
            pltpu.VMEM((hd, tok), low_type),
            pltpu.VMEM((far, count, 2, piece_keys, hd), cluster_kv.dtype),
            pltpu.VMEM((far, groups, hd, cols), low_type),
            pltpu.VMEM((2, keys, hd), low_type),
            pltpu.VMEM((2, hd, keys), low_type),
            pltpu.VMEM((2, groups, 1, cols), jnp.float32),
            pltpu.VMEM((2, groups, 1, cols), jnp.float32),
            pltpu.VMEM((2, groups, hd, cols), jnp.float32),
            pltpu.VMEM((far, groups, hd, cols), low_type),
            pltpu.VMEM((far, groups, 2, cols), jnp.float32),
            pltpu.VMEM((far + 1, groups, hd, cols), low_type),
            pltpu.VMEM((far + 1, groups, 2, cols), jnp.float32),
            pltpu.VMEM((far, groups, tok, depth // groups), low_type),
            pltpu.VMEM((2, depth, columns), w_out.dtype),
            pltpu.VMEM((far, 2, half, wide), jnp.float32),
            pltpu.VMEM((far, half, wide), jnp.float32),
            pltpu.VMEM((far, half, wide), low_type),
            dma((3,)),
            dma,
            dma((far,)),
            dma((2, far)),
            dma((far, groups)),
            dma((far,)),
            dma((far + 1, groups)),
            dma((far,)),
            dma((far + 1, groups)),
            dma((2, far)),
            dma((far, groups)),
            dma,
            dma((groups,)),
            dma,
            dma((groups,)),
            dma,
            dma((far,)),
            dma,
            dma((far,)),
        ],
        compiler_params=pltpu.CompilerParams(
            collective_id=0, has_side_effects=True, vmem_limit_bytes=62 * 2**20),
        name="serve",
    )(cluster_ids[:, 0].T, piece_slot, cluster_len, queries, new_keys[:, 0], new_values[:, 0], cluster_kv, w_out)


def solution(mesh):
    return jax.shard_map(
        local,
        mesh=mesh,
        in_specs=(
            P(("groups", "req"), "head", None),
            P(("groups", "req"), "head", None),
            P(("groups", "req"), "head", None),
            P(("groups", "req"), "head", None, None, None),
            P("groups"),
            P("groups", None),
            P("groups", "head", None),
            P("head", "req"),
        ),
        out_specs=P(("groups", "req", "head"), None),
        check_vma=False,
    )
```

```python
import functools

import jax
import jax.numpy as jnp
from jax import lax
from jax.experimental import pallas as pl
from jax.experimental.pallas import tpu as pltpu
from jax.sharding import PartitionSpec as P

MESH = pl.DeviceIdType.MESH
NEG = -1e30
LOG2E = 1.4426950408889634


def serve_kernel(far, ids_ref, slot_ref, len_ref, q_ref, k_ref, v_ref, kv_ref, w_ref, out_ref,
                 lim_ref, idx_ref, held, gift, vt, qv, nbr, qt, kb, vb, top, total, acc, mine, mine_st, came, came_st, full, wv, part, got, low,
                 load_sem, kv_send, kv_recv, q_send, q_recv, p_send, p_recv, s_send, s_recv, a_send, a_recv,
                 wy_send, wy_recv, wx_send, wx_recv, part_send, part_recv, out_send, out_recv):
    me = lax.axis_index("req")
    head = lax.axis_index("head")
    grp = lax.axis_index("groups")
    hi, lo = me // 2, me % 2
    end = far - 1
    pair = {"req": me + 1 - 2 * lo}
    twin = {"groups": grp + 1 - 2 * (grp % 2)}
    mate = {"head": 1 - head}

    tok, hd = k_ref.shape
    heads = q_ref.shape[1]
    count, piece_keys = gift.shape[1], gift.shape[3]
    keys = count * piece_keys
    _, groups, _, cols = qt.shape
    sel = ids_ref.shape[0]
    pieces = slot_ref.shape[1]
    per = count // sel
    slots = held.shape[0]
    per_group = cols // tok
    block = min(256, cols)
    factor = hd ** (-0.5) * LOG2E
    half = out_ref.shape[0]
    depth, columns = w_ref.shape
    wide = 2 * columns
    slab = depth // (2 * groups)
    slice_depth = depth // groups

    def at(z):
        return {"req": z * 2 + lo}

    load_kv = pltpu.make_async_copy(kv_ref, held, load_sem.at[0])
    load_w = pltpu.make_async_copy(w_ref, wv.at[lo], load_sem.at[1])
    load_q = pltpu.make_async_copy(q_ref, qv, load_sem.at[2])
    load_q.start()
    load_kv.start()
    load_w.start()

    barrier = pltpu.get_barrier_semaphore()
    for k in range(1, far):
        pl.semaphore_signal(barrier, inc=1, device_id=at(lax.rem(hi + k, far)), device_id_type=MESH)
    for device in (pair, twin, mate):
        pl.semaphore_signal(barrier, inc=1, device_id=device, device_id_type=MESH)

    rising = hi < end - hi
    shorter = jnp.where(rising, hi, end - hi)

    at_end = (hi == 0) | (hi == end)

    ahead = jnp.logical_not(at_end) & (end - 2 * shorter == 1)

    def order(i):
        i = jnp.where(ahead & ((i == 1) | (i == 2)), 3 - i, i)
        n = far - i
        both = n <= 2 * shorter
        d = jnp.where(both, (n + 1) // 2, n - shorter)
        above = jnp.where(both, (n % 2 == 1) == rising, rising)
        return jnp.where((i == 0) | (i == far), hi, jnp.where(above, hi + d, hi - d))

    def q_copy(z, g, to, way):
        return pltpu.make_async_remote_copy(
            src_ref=qt.at[z, g], dst_ref=qt.at[z, g], send_sem=q_send.at[way, z],
            recv_sem=q_recv.at[z, g], device_id=at(to), device_id_type=MESH)

    def a_copy(z, g, to, way):
        return pltpu.make_async_remote_copy(
            src_ref=full.at[z, g], dst_ref=full.at[z, g], send_sem=a_send.at[way, z],
            recv_sem=a_recv.at[z, g], device_id=at(to), device_id_type=MESH)

    halves = 1
    share = count // halves

    def kv_copy(z, n):
        some = pl.ds(n * share, share)
        return pltpu.make_async_remote_copy(
            src_ref=gift.at[z, some], dst_ref=nbr.at[z, some], send_sem=kv_send,
            recv_sem=kv_recv.at[z, n], device_id=pair, device_id_type=MESH)

    def fetch(z, n):
        kv_copy(z, n).wait_recv()
        for j in range(n * share, (n + 1) * share):
            at_j = slice(j * piece_keys, (j + 1) * piece_keys)
            kb[1, at_j] = nbr[z, j, 0]
            vb[1, :, at_j] = nbr[z, j, 1].T

    def w_rows(which, c):
        return pl.ds(pl.multiple_of((which * groups + c) * slab, slab), slab)

    def wy_copy(c, slot):
        rows = w_rows(grp % 2, c)
        return pltpu.make_async_remote_copy(
            src_ref=w_ref.at[rows], dst_ref=wv.at[slot, rows], send_sem=wy_send,
            recv_sem=wy_recv.at[c], device_id=pair, device_id_type=MESH)

    def wx_copy(c, which):
        rows = w_rows(which, c)
        return pltpu.make_async_remote_copy(
            src_ref=wv.at[1 - lo, rows], dst_ref=wv.at[1 - lo, rows], send_sem=wx_send,
            recv_sem=wx_recv.at[c], device_id=twin, device_id_type=MESH)

    def pass_w(c):
        wy_copy(c, 1 - lo).wait_recv()
        wx_copy(c, grp % 2).start()

    def inner(b):
        return jnp.where(hi > b, hi - 1, hi + 1)

    def part_pair(b, g, slot, to):
        return (
            pltpu.make_async_remote_copy(
                src_ref=mine.at[b, g], dst_ref=came.at[slot, g], send_sem=p_send.at[b],
                recv_sem=p_recv.at[slot, g], device_id=at(to), device_id_type=MESH),
            pltpu.make_async_remote_copy(
                src_ref=mine_st.at[b, g], dst_ref=came_st.at[slot, g], send_sem=s_send.at[b],
                recv_sem=s_recv.at[slot, g], device_id=at(to), device_id_type=MESH))

    def part_start(b, g):
        to = inner(b)
        slot = jnp.where((to == b) & (hi > b), far, b)
        for copy in part_pair(b, g, slot, to):
            copy.start()

    def part_wait(b, g, slot):
        for copy in part_pair(b, g, slot, jnp.where(hi < end, hi + 1, hi - 1)):
            copy.wait_recv()

    def find(c, base, also=None):
        locs, lims = [jnp.int32(0)] * per, [jnp.int32(0)] * per
        n = jnp.int32(0)
        fill = len_ref[c]
        for p in range(pieces):
            loc = slot_ref[c, p] - base
            hit = (loc >= 0) & (loc < slots)
            left = fill - p * piece_keys
            for j in range(per):
                take = hit & (n == j)
                locs[j] = jnp.where(take, loc, locs[j])
                lims[j] = jnp.where(take, left, lims[j])
            n = n + hit.astype(jnp.int32)
        return locs, lims

    def plan(z, s):
        c = ids_ref[s, z * 2 + lo]
        locs, lims = find(c, me * slots)
        _, others = find(c, (me + 1 - 2 * lo) * slots)
        for j in range(per):
            idx_ref[z, s * per + j] = locs[j]
            lim_ref[0, z, s * per + j] = lims[j]
            lim_ref[1, z, s * per + j] = others[j]

    def give(z):
        found = []
        for s in range(sel):
            found += find(ids_ref[s, z * 2 + 1 - lo], me * slots)[0]
        return found

    def wrap(z, found):
        for j in range(count):
            gift[z, j] = held[found[j], 0]
        for n in range(halves):
            kv_copy(z, n).start()

    found = give(order(1))
    load_q.wait()
    for h in range(heads):
        at_h = h % per_group
        qt[hi, h // per_group, :, at_h * tok:(at_h + 1) * tok] = qv[:, h, :].T
    pl.semaphore_wait(barrier, far + 2)

    def first(gap):
        return jnp.where((gap == 0) | (2 * gap > groups), groups, 2 * gap)

    def intake(n, g, upper):
        above, below = end - n + 1, n - 1

        @pl.when(upper & (above > hi))
        def _():
            q_copy(above, g, hi, 1).wait_recv()

            @pl.when(hi > 0)
            def _():
                q_copy(above, g, hi - 1, 1).start()

        @pl.when(jnp.logical_not(upper) & (below < hi))
        def _():
            q_copy(below, g, hi, 0).wait_recv()

            @pl.when(hi < end)
            def _():
                q_copy(below, g, hi + 1, 0).start()

    @pl.loop(0, groups)
    def _(g):
        @pl.when((hi < end) & (g < first(hi)))
        def _():
            q_copy(hi, g, hi + 1, 0).start()

        @pl.when((hi > 0) & (g < first(end - hi)))
        def _():
            q_copy(hi, g, hi - 1, 1).start()

    load_kv.wait()
    wrap(order(1), found)

    vt[...] = v_ref[...].T
    for s in range(sel):
        plan(hi, s)
        plan(order(1), s)

    @pl.loop(2, far + 1)
    def _(i):
        z = order(i)
        wrap(z, give(z))

    @pl.loop(0, groups)
    def _(c):
        wy_copy(c, lo).start()

    def begin(g):
        s = jnp.dot(k_ref[...], qt[hi, g], preferred_element_type=jnp.float32)
        u = lax.broadcasted_iota(jnp.int32, s.shape, 0)
        t = lax.broadcasted_iota(jnp.int32, s.shape, 1) % tok
        s = jnp.where(u <= t, s, NEG)
        m = jnp.max(s, axis=0, keepdims=True)
        w = jnp.exp2((s - m) * factor)
        top[0, g] = m
        total[0, g] = jnp.sum(w, axis=0, keepdims=True)
        acc[0, g] = jnp.dot(vt[...], w.astype(jnp.bfloat16), preferred_element_type=jnp.float32)

    def unit(z, parts, slot, g):
        key = lax.broadcasted_iota(jnp.int32, (piece_keys, block), 0)
        steps = [(*part, b) for part in parts for b in range(cols // block)]

        def score(side, src, low_j, high_j, b):
            k = kb[src, low_j * piece_keys:high_j * piece_keys]
            s = jnp.dot(k, qt[z, g, :, b * block:(b + 1) * block], preferred_element_type=jnp.float32)
            return jnp.concatenate(
                [jnp.where(key < lim_ref[side, z, low_j + n], s[n * piece_keys:(n + 1) * piece_keys], NEG)
                 for n in range(high_j - low_j)], axis=0)

        def weigh(src, low_j, high_j, b, s):
            at_b = slice(b * block, (b + 1) * block)
            m_old = top[slot, g, :, at_b]
            m = jnp.maximum(m_old, jnp.max(s, axis=0, keepdims=True))
            keep = jnp.exp2((m_old - m) * factor)
            w = jnp.exp2((s - m) * factor)
            v = vb[src, :, low_j * piece_keys:high_j * piece_keys]
            mixed = jnp.dot(v, w.astype(jnp.bfloat16), preferred_element_type=jnp.float32)
            top[slot, g, :, at_b] = m
            total[slot, g, :, at_b] = total[slot, g, :, at_b] * keep + jnp.sum(w, axis=0, keepdims=True)
            acc[slot, g, :, at_b] = acc[slot, g, :, at_b] * keep + mixed

        s = score(*steps[0])
        for n, (_, *step) in enumerate(steps):
            later = score(*steps[n + 1]) if n + 1 < len(steps) else None
            weigh(*step, s)
            s = later

    def blend(m1, l1, a1, m2, l2, a2):
        m = jnp.maximum(m1, m2)
        f1 = jnp.exp2((m1 - m) * factor)
        f2 = jnp.exp2((m2 - m) * factor)
        return m, l1 * f1 + l2 * f2, a1 * f1 + a2 * f2

    def merge(b, g):
        part_wait(b, g, b)
        m, l, a = blend(
            mine_st[b, g, 0:1], mine_st[b, g, 1:2], mine[b, g].astype(jnp.float32),
            came_st[b, g, 0:1], came_st[b, g, 1:2], came[b, g].astype(jnp.float32))
        mine_st[b, g, 0:1] = m
        mine_st[b, g, 1:2] = l
        mine[b, g] = a.astype(jnp.bfloat16)
        part_start(b, g)

    def absorb(slot, g):
        part_wait(hi, g, slot)
        m, l, a = blend(
            top[0, g], total[0, g], acc[0, g],
            came_st[slot, g, 0:1], came_st[slot, g, 1:2], came[slot, g].astype(jnp.float32))
        top[0, g] = m
        total[0, g] = l
        acc[0, g] = a

    def stage(z, buf):
        for j in range(count):
            at_j = slice(j * piece_keys, (j + 1) * piece_keys)
            loc = idx_ref[z, j]
            kb[buf, at_j] = held[loc, 0, 0]
            vb[buf, :, at_j] = held[loc, 0, 1].T

    @pl.loop(0, far + 1)
    def _(i):
        b = order(i)
        slot = jnp.where(b == hi, 0, 1)
        closing = i == far
        middle = (i > 0) & (i < far)

        low_b = i - 1 - end + hi
        high_b = far + hi - i

        def join(g, fresh):
            @pl.when((low_b >= 0) & (low_b < hi) & (hi < end) & ((low_b == b) == fresh))
            def _():
                merge(low_b, g)

            @pl.when((high_b > hi) & (high_b <= end) & (hi > 0) & ((high_b == b) == fresh))
            def _():
                merge(high_b, g)

        @pl.when(i < far)
        def _():
            stage(b, 0)

        @pl.when((ahead & (i == 0)) | (jnp.logical_not(ahead) & middle) | (middle & (i > 1)))
        def _():
            top[1] = jnp.full_like(top[1], NEG)
            total[1] = jnp.zeros_like(total[1])
            acc[1] = jnp.zeros_like(acc[1])

        @pl.when(ahead & (i == 0))
        def _():
            stage(order(1), 1)

        join(0, False)

        @pl.when(i > 0)
        def _():
            for n in range(halves):
                fetch(b, n)

        @pl.loop(0, groups)
        def _(g):
            @pl.when(at_end & middle)
            def _():
                intake(i, g, hi == 0)

            alone = closing | (ahead & (i == 1))

            @pl.when(g > 0)
            def _():
                join(g, False)

            @pl.when(i == 0)
            def _():
                begin(g)
                unit(b, [(0, 0, 0, count)], slot, g)

            @pl.when(ahead & (i == 0))
            def _():
                intake(1, g, jnp.logical_not(rising))
                unit(order(1), [(0, 1, 0, count)], 1, g)

            @pl.when(alone)
            def _():
                unit(b, [(1, 1, 0, count)], slot, g)

            @pl.when(middle & jnp.logical_not(alone))
            def _():
                unit(b, [(0, 0, 0, count), (1, 1, 0, count)], slot, g)

            @pl.when(middle)
            def _():
                mine_st[b, g, 0:1] = top[1, g]
                mine_st[b, g, 1:2] = total[1, g]
                mine[b, g] = acc[1, g].astype(jnp.bfloat16)

                @pl.when(at_end)
                def _():
                    part_start(b, g)

            join(g, True)

            @pl.when(closing)
            def _():
                @pl.when(hi > 0)
                def _():
                    absorb(hi, g)

                @pl.when(hi < end)
                def _():
                    absorb(far, g)

                o = acc[0, g] / total[0, g]
                for h in range(per_group):
                    full[hi, g, :, h * hd:(h + 1) * hd] = o[:, h * tok:(h + 1) * tok].T.astype(full.dtype)

                @pl.when(hi < end)
                def _():
                    a_copy(hi, g, hi + 1, 0).start()

                @pl.when(hi > 0)
                def _():
                    a_copy(hi, g, hi - 1, 1).start()

                @pl.when(g == groups - 1)
                def _():
                    pass_w(0)

            @pl.when(jnp.logical_not(at_end))
            def _():
                @pl.when((i < end) & jnp.logical_not(ahead & (i == 0)))
                def _():
                    intake(i + 1, g, jnp.logical_not(rising))

                @pl.when((i == 0) & (g > 0))
                def _():
                    intake(1, g - 1, rising)

                @pl.when((i == 1) & (g == 0))
                def _():
                    intake(1, groups - 1, rising)

                @pl.when((i > 0) & (i < end))
                def _():
                    intake(i + 1, g, rising)

        @pl.when(i == 0)
        def _():
            @pl.loop(2, far)
            def _(k):
                for s in range(sel):
                    plan(order(k), s)

        @pl.when(jnp.logical_not(at_end))
        def _():
            @pl.loop(0, groups)
            def _(g):
                @pl.when((i == hi - 1) & (g >= first(hi)))
                def _():
                    q_copy(hi, g, hi + 1, 0).start()

                @pl.when((i == end - hi - 1) & (g >= first(end - hi)))
                def _():
                    q_copy(hi, g, hi - 1, 1).start()

    def part_copy(z):
        return pltpu.make_async_remote_copy(
            src_ref=part.at[z, 1 - head], dst_ref=got.at[z], send_sem=part_send,
            recv_sem=part_recv.at[z], device_id=mate, device_id_type=MESH)

    def out_copy(z, owner):
        return pltpu.make_async_remote_copy(
            src_ref=low.at[z], dst_ref=out_ref.at[:, pl.ds(pl.multiple_of(owner * wide, wide), wide)],
            send_sem=out_send, recv_sem=out_recv.at[owner], device_id=at(z), device_id_type=MESH)

    keep_copy = pltpu.make_async_copy(
        low.at[hi], out_ref.at[:, pl.ds(pl.multiple_of(hi * wide, wide), wide)], load_sem.at[2])

    def compute(z, j):
        at_j = pl.ds(pl.multiple_of(j * columns, columns), columns)
        terms = jnp.dot(full[z, 0], wv[j, 0:slice_depth], preferred_element_type=jnp.float32)
        for g in range(1, groups):
            terms += jnp.dot(full[z, g], wv[j, g * slice_depth:(g + 1) * slice_depth],
                             preferred_element_type=jnp.float32)
        part[z, 0, :, at_j] = terms[:half]
        part[z, 1, :, at_j] = terms[half:]

    def finish(z):
        part_copy(z).wait_recv()
        rows = (part[z, head] + got[z]).astype(out_ref.dtype)

        low[z] = rows

        @pl.when(z == hi)
        def _():
            keep_copy.start()

        @pl.when(z != hi)
        def _():
            out_copy(z, hi).start()

    load_w.wait()
    settle = min(2, end)

    @pl.loop(0, far)
    def _(d):
        @pl.when(d > 0)
        def _():
            @pl.loop(0, groups)
            def _(g):
                @pl.loop(0, 2)
                def _(turn):
                    above = (turn == 0) == rising

                    @pl.when(jnp.logical_not(above) & (hi - d >= 0))
                    def _():
                        a_copy(hi - d, g, hi, 0).wait_recv()

                        @pl.when(hi < end)
                        def _():
                            a_copy(hi - d, g, hi + 1, 0).start()

                    @pl.when(above & (hi + d <= end))
                    def _():
                        a_copy(hi + d, g, hi, 1).wait_recv()

                        @pl.when(hi > 0)
                        def _():
                            a_copy(hi + d, g, hi - 1, 1).start()

                @pl.when((d == 1) & (g < groups - 1))
                def _():
                    pass_w(g + 1)

        def around(reach, act):
            @pl.loop(0, 2)
            def _(side):
                z = hi + reach * (2 * side - 1)

                @pl.when((z >= 0) & (z < far) & ((reach > 0) | (side == 0)))
                def _():
                    act(z)

        def within(act):
            @pl.loop(0, 2 * settle - 1)
            def _(n):
                z = hi - (settle - 1) + n

                @pl.when((z >= 0) & (z < far))
                def _():
                    act(z)

        def rest(z):
            compute(z, 1 - lo)
            part_copy(z).start()

        @pl.when(d == settle)
        def _():
            @pl.loop(0, groups)
            def _(c):
                wx_copy(c, 1 - grp % 2).wait_recv()

            within(rest)

        def whole(z):
            compute(z, lo)

            @pl.when(d >= settle)
            def _():
                rest(z)

        around(d, whole)

        @pl.when(d == settle)
        def _():
            within(finish)

        @pl.when(d > settle)
        def _():
            around(d - 1, finish)

        @pl.when(d == end)
        def _():
            around(d, finish)

    def sent(src, sem):
        pltpu.make_async_remote_copy(
            src_ref=src, dst_ref=src, send_sem=sem, recv_sem=load_sem.at[0],
            device_id=mate, device_id_type=MESH).wait_send()

    sent(w_ref.at[pl.ds(0, groups * slab)], wy_send)
    sent(w_ref.at[pl.ds(0, groups * slab)], wx_send)
    sent(gift, kv_send)
    sent(got, part_send)
    sent(low.at[pl.ds(0, end)], out_send)

    @pl.loop(0, far)
    def _(z):
        @pl.when((z <= hi) & (hi < end))
        def _():
            sent(qt.at[z], q_send.at[0, z])
            sent(full.at[z], a_send.at[0, z])

        @pl.when((z >= hi) & (hi > 0))
        def _():
            sent(qt.at[z], q_send.at[1, z])
            sent(full.at[z], a_send.at[1, z])

        @pl.when(z != hi)
        def _():
            sent(mine.at[z], p_send.at[z])
            sent(mine_st.at[z], s_send.at[z])
            out_copy(z, z).wait_recv()

    keep_copy.wait()


def local(queries, new_keys, new_values, cluster_kv, cluster_len, piece_slot, cluster_ids, w_out):
    peers = lax.axis_size("req")
    far = peers // 2
    tok, heads, hd = queries.shape
    piece_keys = cluster_kv.shape[3]
    pieces = piece_slot.shape[1]
    sel = cluster_ids.shape[2]
    count = sel * (pieces // peers)
    groups = min(4, heads)
    cols = heads * tok // groups
    keys = count * piece_keys
    half = tok // lax.axis_size("head")
    depth, columns = w_out.shape
    wide = 2 * columns
    vmem = pl.BlockSpec(memory_space=pltpu.VMEM)
    smem = pl.BlockSpec(memory_space=pltpu.SMEM)
    any_space = pl.BlockSpec(memory_space=pltpu.HBM)
    low_type, dma = jnp.bfloat16, pltpu.SemaphoreType.DMA
    return pl.pallas_call(
        functools.partial(serve_kernel, far),
        out_shape=jax.ShapeDtypeStruct((half, peers * columns), low_type),
        in_specs=[smem, smem, smem, any_space, vmem, vmem, any_space, any_space],
        out_specs=any_space,
        scratch_shapes=[
            pltpu.SMEM((2, far, count), jnp.int32),
            pltpu.SMEM((far, count), jnp.int32),
            pltpu.VMEM(cluster_kv.shape, cluster_kv.dtype),
            pltpu.VMEM((far, count, 2, piece_keys, hd), cluster_kv.dtype),
            pltpu.VMEM((hd, tok), low_type),
            pltpu.VMEM(queries.shape, low_type),
            pltpu.VMEM((far, count, 2, piece_keys, hd), cluster_kv.dtype),
            pltpu.VMEM((far, groups, hd, cols), low_type),
            pltpu.VMEM((2, keys, hd), low_type),
            pltpu.VMEM((2, hd, keys), low_type),
            pltpu.VMEM((2, groups, 1, cols), jnp.float32),
            pltpu.VMEM((2, groups, 1, cols), jnp.float32),
            pltpu.VMEM((2, groups, hd, cols), jnp.float32),
            pltpu.VMEM((far, groups, hd, cols), low_type),
            pltpu.VMEM((far, groups, 2, cols), jnp.float32),
            pltpu.VMEM((far + 1, groups, hd, cols), low_type),
            pltpu.VMEM((far + 1, groups, 2, cols), jnp.float32),
            pltpu.VMEM((far, groups, tok, depth // groups), low_type),
            pltpu.VMEM((2, depth, columns), w_out.dtype),
            pltpu.VMEM((far, 2, half, wide), jnp.float32),
            pltpu.VMEM((far, half, wide), jnp.float32),
            pltpu.VMEM((far, half, wide), low_type),
            dma((3,)),
            dma,
            dma((far, 1)),
            dma((2, far)),
            dma((far, groups)),
            dma((far,)),
            dma((far + 1, groups)),
            dma((far,)),
            dma((far + 1, groups)),
            dma((2, far)),
            dma((far, groups)),
            dma,
            dma((groups,)),
            dma,
            dma((groups,)),
            dma,
            dma((far,)),
            dma,
            dma((far,)),
        ],
        compiler_params=pltpu.CompilerParams(
            collective_id=0, has_side_effects=True, vmem_limit_bytes=62 * 2**20),
        name="serve",
    )(cluster_ids[:, 0].T, piece_slot, cluster_len, queries, new_keys[:, 0], new_values[:, 0], cluster_kv, w_out)


def solution(mesh):
    return jax.shard_map(
        local,
        mesh=mesh,
        in_specs=(
            P(("groups", "req"), "head", None),
            P(("groups", "req"), "head", None),
            P(("groups", "req"), "head", None),
            P(("groups", "req"), "head", None, None, None),
            P("groups"),
            P("groups", None),
            P("groups", "head", None),
            P("head", "req"),
        ),
        out_specs=P(("groups", "req", "head"), None),
        check_vma=False,
    )
```

```python
import functools

import jax
import jax.numpy as jnp
from jax import lax
from jax.experimental import pallas as pl
from jax.experimental.pallas import tpu as pltpu
from jax.sharding import PartitionSpec as P

MESH = pl.DeviceIdType.MESH
NEG = -1e30
LOG2E = 1.4426950408889634


def serve_kernel(far, ids_ref, slot_ref, len_ref, q_ref, k_ref, v_ref, kv_ref, w_ref, out_ref,
                 lim_ref, idx_ref, held, gift, vt, qv, nbr, qt, kb, vb, top, total, acc, mine, mine_st, came, came_st, full, wv, part, got, low,
                 load_sem, kv_send, kv_recv, q_send, q_recv, p_send, p_recv, s_send, s_recv, a_send, a_recv,
                 wy_send, wy_recv, wx_send, wx_recv, part_send, part_recv, out_send, out_recv):
    me = lax.axis_index("req")
    head = lax.axis_index("head")
    grp = lax.axis_index("groups")
    hi, lo = me // 2, me % 2
    end = far - 1
    pair = {"req": me + 1 - 2 * lo}
    twin = {"groups": grp + 1 - 2 * (grp % 2)}
    mate = {"head": 1 - head}

    tok, hd = k_ref.shape
    heads = q_ref.shape[1]
    count, piece_keys = gift.shape[1], gift.shape[3]
    keys = count * piece_keys
    _, groups, _, cols = qt.shape
    sel = ids_ref.shape[0]
    pieces = slot_ref.shape[1]
    per = count // sel
    slots = held.shape[0]
    per_group = cols // tok
    block = min(256, cols)
    factor = hd ** (-0.5) * LOG2E
    half = out_ref.shape[0]
    depth, columns = w_ref.shape
    wide = 2 * columns
    slab = depth // (2 * groups)
    slice_depth = depth // groups

    def at(z):
        return {"req": z * 2 + lo}

    load_kv = pltpu.make_async_copy(kv_ref, held, load_sem.at[0])
    load_w = pltpu.make_async_copy(w_ref, wv.at[lo], load_sem.at[1])
    load_q = pltpu.make_async_copy(q_ref, qv, load_sem.at[2])
    load_q.start()
    load_kv.start()
    load_w.start()

    barrier = pltpu.get_barrier_semaphore()
    for k in range(1, far):
        pl.semaphore_signal(barrier, inc=1, device_id=at(lax.rem(hi + k, far)), device_id_type=MESH)
    for device in (pair, twin, mate):
        pl.semaphore_signal(barrier, inc=1, device_id=device, device_id_type=MESH)

    rising = hi < end - hi
    shorter = jnp.where(rising, hi, end - hi)

    at_end = (hi == 0) | (hi == end)

    ahead = jnp.logical_not(at_end) & (end - 2 * shorter == 1)

    def order(i):
        i = jnp.where(ahead & ((i == 1) | (i == 2)), 3 - i, i)
        n = far - i
        both = n <= 2 * shorter
        d = jnp.where(both, (n + 1) // 2, n - shorter)
        above = jnp.where(both, (n % 2 == 1) == rising, rising)
        return jnp.where((i == 0) | (i == far), hi, jnp.where(above, hi + d, hi - d))

    def q_copy(z, g, to, way):
        return pltpu.make_async_remote_copy(
            src_ref=qt.at[z, g], dst_ref=qt.at[z, g], send_sem=q_send.at[way, z],
            recv_sem=q_recv.at[z, g], device_id=at(to), device_id_type=MESH)

    def a_copy(z, g, to, way):
        return pltpu.make_async_remote_copy(
            src_ref=full.at[z, g], dst_ref=full.at[z, g], send_sem=a_send.at[way, z],
            recv_sem=a_recv.at[z, g], device_id=at(to), device_id_type=MESH)

    halves = 1
    share = count // halves

    def kv_copy(z, n):
        some = pl.ds(n * share, share)
        return pltpu.make_async_remote_copy(
            src_ref=gift.at[z, some], dst_ref=nbr.at[z, some], send_sem=kv_send,
            recv_sem=kv_recv.at[z, n], device_id=pair, device_id_type=MESH)

    def fetch(z, n):
        kv_copy(z, n).wait_recv()
        for j in range(n * share, (n + 1) * share):
            at_j = slice(j * piece_keys, (j + 1) * piece_keys)
            kb[1, at_j] = nbr[z, j, 0]
            vb[1, :, at_j] = nbr[z, j, 1].T

    def w_rows(which, c):
        return pl.ds(pl.multiple_of((which * groups + c) * slab, slab), slab)

    def wy_copy(c, slot):
        rows = w_rows(grp % 2, c)
        return pltpu.make_async_remote_copy(
            src_ref=w_ref.at[rows], dst_ref=wv.at[slot, rows], send_sem=wy_send,
            recv_sem=wy_recv.at[c], device_id=pair, device_id_type=MESH)

    def wx_copy(c, which):
        rows = w_rows(which, c)
        return pltpu.make_async_remote_copy(
            src_ref=wv.at[1 - lo, rows], dst_ref=wv.at[1 - lo, rows], send_sem=wx_send,
            recv_sem=wx_recv.at[c], device_id=twin, device_id_type=MESH)

    def pass_w(c):
        wy_copy(c, 1 - lo).wait_recv()
        wx_copy(c, grp % 2).start()

    def inner(b):
        return jnp.where(hi > b, hi - 1, hi + 1)

    def part_pair(b, g, slot, to):
        return (
            pltpu.make_async_remote_copy(
                src_ref=mine.at[b, g], dst_ref=came.at[slot, g], send_sem=p_send.at[b],
                recv_sem=p_recv.at[slot, g], device_id=at(to), device_id_type=MESH),
            pltpu.make_async_remote_copy(
                src_ref=mine_st.at[b, g], dst_ref=came_st.at[slot, g], send_sem=s_send.at[b],
                recv_sem=s_recv.at[slot, g], device_id=at(to), device_id_type=MESH))

    def part_start(b, g):
        to = inner(b)
        slot = jnp.where((to == b) & (hi > b), far, b)
        for copy in part_pair(b, g, slot, to):
            copy.start()

    def part_wait(b, g, slot):
        for copy in part_pair(b, g, slot, jnp.where(hi < end, hi + 1, hi - 1)):
            copy.wait_recv()

    def find(c, base, also=None):
        locs, lims = [jnp.int32(0)] * per, [jnp.int32(0)] * per
        n = jnp.int32(0)
        fill = len_ref[c]
        for p in range(pieces):
            loc = slot_ref[c, p] - base
            hit = (loc >= 0) & (loc < slots)
            left = fill - p * piece_keys
            for j in range(per):
                take = hit & (n == j)
                locs[j] = jnp.where(take, loc, locs[j])
                lims[j] = jnp.where(take, left, lims[j])
            n = n + hit.astype(jnp.int32)
        return locs, lims

    def plan(z, s):
        c = ids_ref[s, z * 2 + lo]
        locs, lims = find(c, me * slots)
        _, others = find(c, (me + 1 - 2 * lo) * slots)
        for j in range(per):
            idx_ref[z, s * per + j] = locs[j]
            lim_ref[0, z, s * per + j] = lims[j]
            lim_ref[1, z, s * per + j] = others[j]

    def give(z):
        found = []
        for s in range(sel):
            found += find(ids_ref[s, z * 2 + 1 - lo], me * slots)[0]
        return found

    def wrap(z, found):
        for j in range(count):
            gift[z, j] = held[found[j], 0]
        for n in range(halves):
            kv_copy(z, n).start()

    found = give(order(1))
    load_q.wait()
    for h in range(heads):
        at_h = h % per_group
        qt[hi, h // per_group, :, at_h * tok:(at_h + 1) * tok] = qv[:, h, :].T
    pl.semaphore_wait(barrier, far + 2)

    def first(gap):
        return jnp.where((gap == 0) | (2 * gap > groups), groups, 2 * gap)

    def intake(n, g, upper):
        above, below = end - n + 1, n - 1

        @pl.when(upper & (above > hi))
        def _():
            q_copy(above, g, hi, 1).wait_recv()

            @pl.when(hi > 0)
            def _():
                q_copy(above, g, hi - 1, 1).start()

        @pl.when(jnp.logical_not(upper) & (below < hi))
        def _():
            q_copy(below, g, hi, 0).wait_recv()

            @pl.when(hi < end)
            def _():
                q_copy(below, g, hi + 1, 0).start()

    @pl.loop(0, groups)
    def _(g):
        @pl.when((hi < end) & (g < first(hi)))
        def _():
            q_copy(hi, g, hi + 1, 0).start()

        @pl.when((hi > 0) & (g < first(end - hi)))
        def _():
            q_copy(hi, g, hi - 1, 1).start()

    load_kv.wait()
    wrap(order(1), found)

    vt[...] = v_ref[...].T
    for s in range(sel):
        plan(hi, s)
        plan(order(1), s)

    @pl.loop(2, far + 1)
    def _(i):
        z = order(i)
        wrap(z, give(z))

    @pl.loop(0, groups)
    def _(c):
        wy_copy(c, lo).start()

    def begin(g):
        s = jnp.dot(k_ref[...], qt[hi, g], preferred_element_type=jnp.float32)
        u = lax.broadcasted_iota(jnp.int32, s.shape, 0)
        t = lax.broadcasted_iota(jnp.int32, s.shape, 1) % tok
        s = jnp.where(u <= t, s, NEG)
        m = jnp.max(s, axis=0, keepdims=True)
        w = jnp.exp2((s - m) * factor)
        top[0, g] = m
        total[0, g] = jnp.sum(w, axis=0, keepdims=True)
        acc[0, g] = jnp.dot(vt[...], w.astype(jnp.bfloat16), preferred_element_type=jnp.float32)

    def unit(z, parts, slot, g):
        key = lax.broadcasted_iota(jnp.int32, (piece_keys, block), 0)
        steps = [(*part, b) for part in parts for b in range(cols // block)]

        def score(side, src, low_j, high_j, b):
            k = kb[src, low_j * piece_keys:high_j * piece_keys]
            s = jnp.dot(k, qt[z, g, :, b * block:(b + 1) * block], preferred_element_type=jnp.float32)
            return jnp.concatenate(
                [jnp.where(key < lim_ref[side, z, low_j + n], s[n * piece_keys:(n + 1) * piece_keys], NEG)
                 for n in range(high_j - low_j)], axis=0)

        def weigh(src, low_j, high_j, b, s):
            at_b = slice(b * block, (b + 1) * block)
            m_old = top[slot, g, :, at_b]
            m = jnp.maximum(m_old, jnp.max(s, axis=0, keepdims=True))
            keep = jnp.exp2((m_old - m) * factor)
            w = jnp.exp2((s - m) * factor)
            v = vb[src, :, low_j * piece_keys:high_j * piece_keys]
            mixed = jnp.dot(v, w.astype(jnp.bfloat16), preferred_element_type=jnp.float32)
            top[slot, g, :, at_b] = m
            total[slot, g, :, at_b] = total[slot, g, :, at_b] * keep + jnp.sum(w, axis=0, keepdims=True)
            acc[slot, g, :, at_b] = acc[slot, g, :, at_b] * keep + mixed

        s = score(*steps[0])
        for n, (_, *step) in enumerate(steps):
            later = score(*steps[n + 1]) if n + 1 < len(steps) else None
            weigh(*step, s)
            s = later

    def blend(m1, l1, a1, m2, l2, a2):
        m = jnp.maximum(m1, m2)
        f1 = jnp.exp2((m1 - m) * factor)
        f2 = jnp.exp2((m2 - m) * factor)
        return m, l1 * f1 + l2 * f2, a1 * f1 + a2 * f2

    def merge(b, g):
        part_wait(b, g, b)
        m, l, a = blend(
            mine_st[b, g, 0:1], mine_st[b, g, 1:2], mine[b, g].astype(jnp.float32),
            came_st[b, g, 0:1], came_st[b, g, 1:2], came[b, g].astype(jnp.float32))
        mine_st[b, g, 0:1] = m
        mine_st[b, g, 1:2] = l
        mine[b, g] = a.astype(jnp.bfloat16)
        part_start(b, g)

    def absorb(slot, g):
        part_wait(hi, g, slot)
        m, l, a = blend(
            top[0, g], total[0, g], acc[0, g],
            came_st[slot, g, 0:1], came_st[slot, g, 1:2], came[slot, g].astype(jnp.float32))
        top[0, g] = m
        total[0, g] = l
        acc[0, g] = a

    def stage(z, buf):
        for j in range(count):
            at_j = slice(j * piece_keys, (j + 1) * piece_keys)
            loc = idx_ref[z, j]
            kb[buf, at_j] = held[loc, 0, 0]
            vb[buf, :, at_j] = held[loc, 0, 1].T

    @pl.loop(0, far + 1)
    def _(i):
        b = order(i)
        slot = jnp.where(b == hi, 0, 1)
        closing = i == far
        middle = (i > 0) & (i < far)

        low_b = i - 1 - end + hi
        high_b = far + hi - i

        def join(g, fresh):
            @pl.when((low_b >= 0) & (low_b < hi) & (hi < end) & ((low_b == b) == fresh))
            def _():
                merge(low_b, g)

            @pl.when((high_b > hi) & (high_b <= end) & (hi > 0) & ((high_b == b) == fresh))
            def _():
                merge(high_b, g)

        @pl.when(i < far)
        def _():
            stage(b, 0)

        @pl.when((ahead & (i == 0)) | (jnp.logical_not(ahead) & middle) | (middle & (i > 1)))
        def _():
            top[1] = jnp.full_like(top[1], NEG)
            total[1] = jnp.zeros_like(total[1])
            acc[1] = jnp.zeros_like(acc[1])

        @pl.when(ahead & (i == 0))
        def _():
            stage(order(1), 1)

        join(0, False)

        @pl.when(i > 0)
        def _():
            for n in range(halves):
                fetch(b, n)

        @pl.loop(0, groups)
        def _(g):
            @pl.when(at_end & middle)
            def _():
                intake(i, g, hi == 0)

            alone = closing | (ahead & (i == 1))

            @pl.when(g > 0)
            def _():
                join(g, False)

            @pl.when(i == 0)
            def _():
                begin(g)
                unit(b, [(0, 0, 0, count)], slot, g)

            @pl.when(ahead & (i == 0))
            def _():
                intake(1, g, jnp.logical_not(rising))
                unit(order(1), [(0, 1, 0, count)], 1, g)

            @pl.when(alone)
            def _():
                unit(b, [(1, 1, 0, count)], slot, g)

            @pl.when(middle & jnp.logical_not(alone))
            def _():
                unit(b, [(0, 0, 0, count), (1, 1, 0, count)], slot, g)

            @pl.when(middle)
            def _():
                mine_st[b, g, 0:1] = top[1, g]
                mine_st[b, g, 1:2] = total[1, g]
                mine[b, g] = acc[1, g].astype(jnp.bfloat16)

                @pl.when(at_end)
                def _():
                    part_start(b, g)

            join(g, True)

            @pl.when(closing)
            def _():
                @pl.when(hi > 0)
                def _():
                    absorb(hi, g)

                @pl.when(hi < end)
                def _():
                    absorb(far, g)

                o = acc[0, g] / total[0, g]
                for h in range(per_group):
                    full[hi, g, :, h * hd:(h + 1) * hd] = o[:, h * tok:(h + 1) * tok].T.astype(full.dtype)

                @pl.when(hi < end)
                def _():
                    a_copy(hi, g, hi + 1, 0).start()

                @pl.when(hi > 0)
                def _():
                    a_copy(hi, g, hi - 1, 1).start()

                @pl.when(g == groups - 1)
                def _():
                    pass_w(0)

            @pl.when(jnp.logical_not(at_end))
            def _():
                @pl.when((i < end) & jnp.logical_not(ahead & (i == 0)))
                def _():
                    intake(i + 1, g, jnp.logical_not(rising))

                @pl.when((i == 0) & (g > 0))
                def _():
                    intake(1, g - 1, rising)

                @pl.when((i == 1) & (g == 0))
                def _():
                    intake(1, groups - 1, rising)

                @pl.when((i > 0) & (i < end))
                def _():
                    intake(i + 1, g, rising)

        @pl.when(i == 0)
        def _():
            @pl.loop(2, far)
            def _(k):
                for s in range(sel):
                    plan(order(k), s)

        @pl.when(jnp.logical_not(at_end))
        def _():
            @pl.loop(0, groups)
            def _(g):
                @pl.when((i == hi - 1) & (g >= first(hi)))
                def _():
                    q_copy(hi, g, hi + 1, 0).start()

                @pl.when((i == end - hi - 1) & (g >= first(end - hi)))
                def _():
                    q_copy(hi, g, hi - 1, 1).start()

    def part_copy(z):
        return pltpu.make_async_remote_copy(
            src_ref=part.at[z, 1 - head], dst_ref=got.at[z], send_sem=part_send,
            recv_sem=part_recv.at[z], device_id=mate, device_id_type=MESH)

    def out_copy(z, owner):
        return pltpu.make_async_remote_copy(
            src_ref=low.at[z], dst_ref=out_ref.at[:, pl.ds(pl.multiple_of(owner * wide, wide), wide)],
            send_sem=out_send, recv_sem=out_recv.at[owner], device_id=at(z), device_id_type=MESH)

    keep_copy = pltpu.make_async_copy(
        low.at[hi], out_ref.at[:, pl.ds(pl.multiple_of(hi * wide, wide), wide)], load_sem.at[2])

    def compute(z, j):
        at_j = pl.ds(pl.multiple_of(j * columns, columns), columns)
        terms = jnp.dot(full[z, 0], wv[j, 0:slice_depth], preferred_element_type=jnp.float32)
        for g in range(1, groups):
            terms += jnp.dot(full[z, g], wv[j, g * slice_depth:(g + 1) * slice_depth],
                             preferred_element_type=jnp.float32)
        part[z, 0, :, at_j] = terms[:half]
        part[z, 1, :, at_j] = terms[half:]

    def finish(z):
        part_copy(z).wait_recv()
        rows = (part[z, head] + got[z]).astype(out_ref.dtype)

        low[z] = rows

        @pl.when(z == hi)
        def _():
            keep_copy.start()

        @pl.when(z != hi)
        def _():
            out_copy(z, hi).start()

    load_w.wait()
    settle = min(2, end)

    @pl.loop(0, far)
    def _(d):
        @pl.when(d > 0)
        def _():
            @pl.loop(0, groups)
            def _(g):
                @pl.loop(0, 2)
                def _(turn):
                    above = (turn == 0) == rising

                    @pl.when(jnp.logical_not(above) & (hi - d >= 0))
                    def _():
                        a_copy(hi - d, g, hi, 0).wait_recv()

                        @pl.when(hi < end)
                        def _():
                            a_copy(hi - d, g, hi + 1, 0).start()

                    @pl.when(above & (hi + d <= end))
                    def _():
                        a_copy(hi + d, g, hi, 1).wait_recv()

                        @pl.when(hi > 0)
                        def _():
                            a_copy(hi + d, g, hi - 1, 1).start()

                @pl.when((d == 1) & (g < groups - 1))
                def _():
                    pass_w(g + 1)

        def around(reach, act):
            @pl.loop(0, 2)
            def _(side):
                z = hi + reach * (2 * side - 1)

                @pl.when((z >= 0) & (z < far) & ((reach > 0) | (side == 0)))
                def _():
                    act(z)

        def within(act):
            @pl.loop(0, 2 * settle - 1)
            def _(n):
                z = hi - (settle - 1) + n

                @pl.when((z >= 0) & (z < far))
                def _():
                    act(z)

        def rest(z):
            compute(z, 1 - lo)
            part_copy(z).start()

        @pl.when(d == settle)
        def _():
            @pl.loop(0, groups)
            def _(c):
                wx_copy(c, 1 - grp % 2).wait_recv()

            within(rest)

        def whole(z):
            compute(z, lo)

            @pl.when(d >= settle)
            def _():
                rest(z)

        around(d, whole)

        @pl.when(d == settle)
        def _():
            within(finish)

        @pl.when(d > settle)
        def _():
            around(d - 1, finish)

        @pl.when(d == end)
        def _():
            around(d, finish)

    def sent(src, sem):
        pltpu.make_async_remote_copy(
            src_ref=src, dst_ref=src, send_sem=sem, recv_sem=load_sem.at[0],
            device_id=mate, device_id_type=MESH).wait_send()

    sent(w_ref.at[pl.ds(0, groups * slab)], wy_send)
    sent(w_ref.at[pl.ds(0, groups * slab)], wx_send)
    sent(gift, kv_send)
    sent(got, part_send)
    sent(low.at[pl.ds(0, end)], out_send)

    @pl.loop(0, far)
    def _(z):
        @pl.when((z <= hi) & (hi < end))
        def _():
            sent(qt.at[z], q_send.at[0, z])
            sent(full.at[z], a_send.at[0, z])

        @pl.when((z >= hi) & (hi > 0))
        def _():
            sent(qt.at[z], q_send.at[1, z])
            sent(full.at[z], a_send.at[1, z])

        @pl.when(z != hi)
        def _():
            sent(mine.at[z], p_send.at[z])
            sent(mine_st.at[z], s_send.at[z])
            out_copy(z, z).wait_recv()

    keep_copy.wait()


def local(queries, new_keys, new_values, cluster_kv, cluster_len, piece_slot, cluster_ids, w_out):
    peers = lax.axis_size("req")
    far = peers // 2
    tok, heads, hd = queries.shape
    piece_keys = cluster_kv.shape[3]
    pieces = piece_slot.shape[1]
    sel = cluster_ids.shape[2]
    count = sel * (pieces // peers)
    groups = min(4, heads)
    cols = heads * tok // groups
    keys = count * piece_keys
    half = tok // lax.axis_size("head")
    depth, columns = w_out.shape
    wide = 2 * columns
    vmem = pl.BlockSpec(memory_space=pltpu.VMEM)
    smem = pl.BlockSpec(memory_space=pltpu.SMEM)
    any_space = pl.BlockSpec(memory_space=pltpu.HBM)
    low_type, dma = jnp.bfloat16, pltpu.SemaphoreType.DMA
    return pl.pallas_call(
        functools.partial(serve_kernel, far),
        out_shape=jax.ShapeDtypeStruct((half, peers * columns), low_type),
        in_specs=[smem, smem, smem, any_space, vmem, vmem, any_space, any_space],
        out_specs=any_space,
        scratch_shapes=[
            pltpu.SMEM((2, far, count), jnp.int32),
            pltpu.SMEM((far, count), jnp.int32),
            pltpu.VMEM(cluster_kv.shape, cluster_kv.dtype),
            pltpu.VMEM((far, count, 2, piece_keys, hd), cluster_kv.dtype),
            pltpu.VMEM((hd, tok), low_type),
            pltpu.VMEM(queries.shape, low_type),
            pltpu.VMEM((far, count, 2, piece_keys, hd), cluster_kv.dtype),
            pltpu.VMEM((far, groups, hd, cols), low_type),
            pltpu.VMEM((2, keys, hd), low_type),
            pltpu.VMEM((2, hd, keys), low_type),
            pltpu.VMEM((2, groups, 1, cols), jnp.float32),
            pltpu.VMEM((2, groups, 1, cols), jnp.float32),
            pltpu.VMEM((2, groups, hd, cols), jnp.float32),
            pltpu.VMEM((far, groups, hd, cols), low_type),
            pltpu.VMEM((far, groups, 2, cols), jnp.float32),
            pltpu.VMEM((far + 1, groups, hd, cols), low_type),
            pltpu.VMEM((far + 1, groups, 2, cols), jnp.float32),
            pltpu.VMEM((far, groups, tok, depth // groups), low_type),
            pltpu.VMEM((2, depth, columns), w_out.dtype),
            pltpu.VMEM((far, 2, half, wide), jnp.float32),
            pltpu.VMEM((far, half, wide), jnp.float32),
            pltpu.VMEM((far, half, wide), low_type),
            dma((3,)),
            dma,
            dma((far, 1)),
            dma((2, far)),
            dma((far, groups)),
            dma((far,)),
            dma((far + 1, groups)),
            dma((far,)),
            dma((far + 1, groups)),
            dma((2, far)),
            dma((far, groups)),
            dma,
            dma((groups,)),
            dma,
            dma((groups,)),
            dma,
            dma((far,)),
            dma,
            dma((far,)),
        ],
        compiler_params=pltpu.CompilerParams(
            collective_id=0, has_side_effects=True, vmem_limit_bytes=50 * 2**20),
        name="serve",
    )(*(pltpu.with_memory_space_constraint(x, pltpu.HBM) for x in (
        cluster_ids[:, 0].T, piece_slot, cluster_len, queries, new_keys[:, 0], new_values[:, 0], cluster_kv, w_out)))


def solution(mesh):
    return jax.shard_map(
        local,
        mesh=mesh,
        in_specs=(
            P(("groups", "req"), "head", None),
            P(("groups", "req"), "head", None),
            P(("groups", "req"), "head", None),
            P(("groups", "req"), "head", None, None, None),
            P("groups"),
            P("groups", None),
            P("groups", "head", None),
            P("head", "req"),
        ),
        out_specs=P(("groups", "req", "head"), None),
        check_vma=False,
    )
```

```python
import functools

import jax
import jax.numpy as jnp
from jax import lax
from jax.experimental import pallas as pl
from jax.experimental.pallas import tpu as pltpu
from jax.sharding import PartitionSpec as P

MESH = pl.DeviceIdType.MESH
NEG = -1e30
LOG2E = 1.4426950408889634


def serve_kernel(far, ids_ref, slot_ref, len_ref, q_ref, k_ref, v_ref, kv_ref, w_ref, out_ref,
                 lim_ref, idx_ref, held, gift, vt, qv, new, nbr, qt, kb, vb, top, total, acc, mine, mine_st, came, came_st, full, wv, part, got, low,
                 load_sem, kv_send, kv_recv, q_send, q_recv, p_send, p_recv, s_send, s_recv, a_send, a_recv,
                 wy_send, wy_recv, wx_send, wx_recv, part_send, part_recv, out_send, out_recv):
    me = lax.axis_index("req")
    head = lax.axis_index("head")
    grp = lax.axis_index("groups")
    hi, lo = me // 2, me % 2
    end = far - 1
    pair = {"req": me + 1 - 2 * lo}
    twin = {"groups": grp + 1 - 2 * (grp % 2)}
    mate = {"head": 1 - head}

    tok, hd = k_ref.shape
    heads = q_ref.shape[1]
    count, piece_keys = gift.shape[1], gift.shape[3]
    keys = count * piece_keys
    _, groups, _, cols = qt.shape
    sel = ids_ref.shape[0]
    pieces = slot_ref.shape[1]
    per = count // sel
    slots = held.shape[0]
    per_group = cols // tok
    block = min(256, cols)
    factor = hd ** (-0.5) * LOG2E
    half = out_ref.shape[0]
    depth, columns = w_ref.shape
    wide = 2 * columns
    slab = depth // (2 * groups)
    slice_depth = depth // groups

    def at(z):
        return {"req": z * 2 + lo}

    load_kv = pltpu.make_async_copy(kv_ref, held, load_sem.at[0])
    load_w = pltpu.make_async_copy(w_ref, wv.at[lo], load_sem.at[1])
    load_q = pltpu.make_async_copy(q_ref, qv, load_sem.at[2])
    load_k = pltpu.make_async_copy(k_ref, new.at[0], load_sem.at[3])
    load_v = pltpu.make_async_copy(v_ref, new.at[1], load_sem.at[4])
    load_q.start()
    load_kv.start()
    load_k.start()
    load_v.start()
    load_w.start()

    barrier = pltpu.get_barrier_semaphore()
    for k in range(1, far):
        pl.semaphore_signal(barrier, inc=1, device_id=at(lax.rem(hi + k, far)), device_id_type=MESH)
    for device in (pair, twin, mate):
        pl.semaphore_signal(barrier, inc=1, device_id=device, device_id_type=MESH)

    rising = hi < end - hi
    shorter = jnp.where(rising, hi, end - hi)

    at_end = (hi == 0) | (hi == end)

    ahead = jnp.logical_not(at_end) & (end - 2 * shorter == 1)

    def order(i):
        i = jnp.where(ahead & ((i == 1) | (i == 2)), 3 - i, i)
        n = far - i
        both = n <= 2 * shorter
        d = jnp.where(both, (n + 1) // 2, n - shorter)
        above = jnp.where(both, (n % 2 == 1) == rising, rising)
        return jnp.where((i == 0) | (i == far), hi, jnp.where(above, hi + d, hi - d))

    def q_copy(z, g, to, way):
        return pltpu.make_async_remote_copy(
            src_ref=qt.at[z, g], dst_ref=qt.at[z, g], send_sem=q_send.at[way, z],
            recv_sem=q_recv.at[z, g], device_id=at(to), device_id_type=MESH)

    def a_copy(z, g, to, way):
        return pltpu.make_async_remote_copy(
            src_ref=full.at[z, g], dst_ref=full.at[z, g], send_sem=a_send.at[way, z],
            recv_sem=a_recv.at[z, g], device_id=at(to), device_id_type=MESH)

    halves = 1
    share = count // halves

    def kv_copy(z, n):
        some = pl.ds(n * share, share)
        return pltpu.make_async_remote_copy(
            src_ref=gift.at[z, some], dst_ref=nbr.at[z, some], send_sem=kv_send,
            recv_sem=kv_recv.at[z, n], device_id=pair, device_id_type=MESH)

    def fetch(z, n):
        kv_copy(z, n).wait_recv()
        for j in range(n * share, (n + 1) * share):
            at_j = slice(j * piece_keys, (j + 1) * piece_keys)
            kb[1, at_j] = nbr[z, j, 0]
            vb[1, :, at_j] = nbr[z, j, 1].T

    def w_rows(which, c):
        return pl.ds(pl.multiple_of((which * groups + c) * slab, slab), slab)

    def wy_copy(c, slot):
        rows = w_rows(grp % 2, c)
        return pltpu.make_async_remote_copy(
            src_ref=w_ref.at[rows], dst_ref=wv.at[slot, rows], send_sem=wy_send,
            recv_sem=wy_recv.at[c], device_id=pair, device_id_type=MESH)

    def wx_copy(c, which):
        rows = w_rows(which, c)
        return pltpu.make_async_remote_copy(
            src_ref=wv.at[1 - lo, rows], dst_ref=wv.at[1 - lo, rows], send_sem=wx_send,
            recv_sem=wx_recv, device_id=twin, device_id_type=MESH)

    def pass_w(c):
        wy_copy(c, 1 - lo).wait_recv()
        wx_copy(c, grp % 2).start()

    def inner(b):
        return jnp.where(hi > b, hi - 1, hi + 1)

    def part_pair(b, g, slot, to):
        return (
            pltpu.make_async_remote_copy(
                src_ref=mine.at[b, g], dst_ref=came.at[slot, g], send_sem=p_send.at[b],
                recv_sem=p_recv.at[slot, g], device_id=at(to), device_id_type=MESH),
            pltpu.make_async_remote_copy(
                src_ref=mine_st.at[b, g], dst_ref=came_st.at[slot, g], send_sem=s_send.at[b],
                recv_sem=s_recv.at[slot, g], device_id=at(to), device_id_type=MESH))

    def part_start(b, g):
        to = inner(b)
        slot = jnp.where((to == b) & (hi > b), far, b)
        for copy in part_pair(b, g, slot, to):
            copy.start()

    def part_wait(b, g, slot):
        for copy in part_pair(b, g, slot, jnp.where(hi < end, hi + 1, hi - 1)):
            copy.wait_recv()

    def find(c, base, also=None):
        locs, lims = [jnp.int32(0)] * per, [jnp.int32(0)] * per
        n = jnp.int32(0)
        fill = len_ref[c]
        for p in range(pieces):
            loc = slot_ref[c, p] - base
            hit = (loc >= 0) & (loc < slots)
            left = fill - p * piece_keys
            for j in range(per):
                take = hit & (n == j)
                locs[j] = jnp.where(take, loc, locs[j])
                lims[j] = jnp.where(take, left, lims[j])
            n = n + hit.astype(jnp.int32)
        return locs, lims

    def plan(z, s):
        c = ids_ref[s, z * 2 + lo]
        locs, lims = find(c, me * slots)
        _, others = find(c, (me + 1 - 2 * lo) * slots)
        for j in range(per):
            idx_ref[z, s * per + j] = locs[j]
            lim_ref[0, z, s * per + j] = lims[j]
            lim_ref[1, z, s * per + j] = others[j]

    def give(z):
        found = []
        for s in range(sel):
            found += find(ids_ref[s, z * 2 + 1 - lo], me * slots)[0]
        return found

    def wrap(z, found):
        for j in range(count):
            gift[z, j] = held[found[j], 0]
        for n in range(halves):
            kv_copy(z, n).start()

    found = give(order(1))
    load_q.wait()
    for h in range(heads):
        at_h = h % per_group
        qt[hi, h // per_group, :, at_h * tok:(at_h + 1) * tok] = qv[:, h, :].T
    pl.semaphore_wait(barrier, far + 2)

    def first(gap):
        return jnp.where((gap == 0) | (2 * gap > groups), groups, 2 * gap)

    def intake(n, g, upper):
        above, below = end - n + 1, n - 1

        @pl.when(upper & (above > hi))
        def _():
            q_copy(above, g, hi, 1).wait_recv()

            @pl.when(hi > 0)
            def _():
                q_copy(above, g, hi - 1, 1).start()

        @pl.when(jnp.logical_not(upper) & (below < hi))
        def _():
            q_copy(below, g, hi, 0).wait_recv()

            @pl.when(hi < end)
            def _():
                q_copy(below, g, hi + 1, 0).start()

    @pl.loop(0, groups)
    def _(g):
        @pl.when((hi < end) & (g < first(hi)))
        def _():
            q_copy(hi, g, hi + 1, 0).start()

        @pl.when((hi > 0) & (g < first(end - hi)))
        def _():
            q_copy(hi, g, hi - 1, 1).start()

    load_kv.wait()
    wrap(order(1), found)

    load_k.wait()
    load_v.wait()
    vt[...] = new[1].T
    for s in range(sel):
        plan(hi, s)
        plan(order(1), s)

    @pl.loop(2, far + 1)
    def _(i):
        z = order(i)
        wrap(z, give(z))

    @pl.loop(0, groups)
    def _(c):
        wy_copy(c, lo).start()

    def begin(g):
        s = jnp.dot(new[0], qt[hi, g], preferred_element_type=jnp.float32)
        u = lax.broadcasted_iota(jnp.int32, s.shape, 0)
        t = lax.broadcasted_iota(jnp.int32, s.shape, 1) % tok
        s = jnp.where(u <= t, s, NEG)
        m = jnp.max(s, axis=0, keepdims=True)
        w = jnp.exp2((s - m) * factor)
        top[0, g] = m
        total[0, g] = jnp.sum(w, axis=0, keepdims=True)
        acc[0, g] = jnp.dot(vt[...], w.astype(jnp.bfloat16), preferred_element_type=jnp.float32)

    def unit(z, parts, slot, g):
        key = lax.broadcasted_iota(jnp.int32, (piece_keys, block), 0)
        steps = [(*part, b) for part in parts for b in range(cols // block)]

        def score(side, src, low_j, high_j, b):
            k = kb[src, low_j * piece_keys:high_j * piece_keys]
            s = jnp.dot(k, qt[z, g, :, b * block:(b + 1) * block], preferred_element_type=jnp.float32)
            return jnp.concatenate(
                [jnp.where(key < lim_ref[side, z, low_j + n], s[n * piece_keys:(n + 1) * piece_keys], NEG)
                 for n in range(high_j - low_j)], axis=0)

        def weigh(src, low_j, high_j, b, s):
            at_b = slice(b * block, (b + 1) * block)
            m_old = top[slot, g, :, at_b]
            m = jnp.maximum(m_old, jnp.max(s, axis=0, keepdims=True))
            keep = jnp.exp2((m_old - m) * factor)
            w = jnp.exp2((s - m) * factor)
            v = vb[src, :, low_j * piece_keys:high_j * piece_keys]
            mixed = jnp.dot(v, w.astype(jnp.bfloat16), preferred_element_type=jnp.float32)
            top[slot, g, :, at_b] = m
            total[slot, g, :, at_b] = total[slot, g, :, at_b] * keep + jnp.sum(w, axis=0, keepdims=True)
            acc[slot, g, :, at_b] = acc[slot, g, :, at_b] * keep + mixed

        s = score(*steps[0])
        for n, (_, *step) in enumerate(steps):
            later = score(*steps[n + 1]) if n + 1 < len(steps) else None
            weigh(*step, s)
            s = later

    def blend(m1, l1, a1, m2, l2, a2):
        m = jnp.maximum(m1, m2)
        f1 = jnp.exp2((m1 - m) * factor)
        f2 = jnp.exp2((m2 - m) * factor)
        return m, l1 * f1 + l2 * f2, a1 * f1 + a2 * f2

    def merge(b, g):
        part_wait(b, g, b)
        m, l, a = blend(
            mine_st[b, g, 0:1], mine_st[b, g, 1:2], mine[b, g].astype(jnp.float32),
            came_st[b, g, 0:1], came_st[b, g, 1:2], came[b, g].astype(jnp.float32))
        mine_st[b, g, 0:1] = m
        mine_st[b, g, 1:2] = l
        mine[b, g] = a.astype(jnp.bfloat16)
        part_start(b, g)

    def absorb(slot, g):
        part_wait(hi, g, slot)
        m, l, a = blend(
            top[0, g], total[0, g], acc[0, g],
            came_st[slot, g, 0:1], came_st[slot, g, 1:2], came[slot, g].astype(jnp.float32))
        top[0, g] = m
        total[0, g] = l
        acc[0, g] = a

    def stage(z, buf):
        for j in range(count):
            at_j = slice(j * piece_keys, (j + 1) * piece_keys)
            loc = idx_ref[z, j]
            kb[buf, at_j] = held[loc, 0, 0]
            vb[buf, :, at_j] = held[loc, 0, 1].T

    @pl.loop(0, far + 1)
    def _(i):
        b = order(i)
        slot = jnp.where(b == hi, 0, 1)
        closing = i == far
        middle = (i > 0) & (i < far)

        low_b = i - 1 - end + hi
        high_b = far + hi - i

        def join(g, fresh):
            @pl.when((low_b >= 0) & (low_b < hi) & (hi < end) & ((low_b == b) == fresh))
            def _():
                merge(low_b, g)

            @pl.when((high_b > hi) & (high_b <= end) & (hi > 0) & ((high_b == b) == fresh))
            def _():
                merge(high_b, g)

        @pl.when(i < far)
        def _():
            stage(b, 0)

        @pl.when((ahead & (i == 0)) | (jnp.logical_not(ahead) & middle) | (middle & (i > 1)))
        def _():
            top[1] = jnp.full_like(top[1], NEG)
            total[1] = jnp.zeros_like(total[1])
            acc[1] = jnp.zeros_like(acc[1])

        @pl.when(ahead & (i == 0))
        def _():
            stage(order(1), 1)

        join(0, False)

        @pl.when(i > 0)
        def _():
            for n in range(halves):
                fetch(b, n)

        @pl.loop(0, groups)
        def _(g):
            @pl.when(at_end & middle)
            def _():
                intake(i, g, hi == 0)

            alone = closing | (ahead & (i == 1))

            @pl.when(g > 0)
            def _():
                join(g, False)

            @pl.when(i == 0)
            def _():
                begin(g)
                unit(b, [(0, 0, 0, count)], slot, g)

            @pl.when(ahead & (i == 0))
            def _():
                intake(1, g, jnp.logical_not(rising))
                unit(order(1), [(0, 1, 0, count)], 1, g)

            @pl.when(alone)
            def _():
                unit(b, [(1, 1, 0, count)], slot, g)

            @pl.when(middle & jnp.logical_not(alone))
            def _():
                unit(b, [(0, 0, 0, count), (1, 1, 0, count)], slot, g)

            @pl.when(middle)
            def _():
                mine_st[b, g, 0:1] = top[1, g]
                mine_st[b, g, 1:2] = total[1, g]
                mine[b, g] = acc[1, g].astype(jnp.bfloat16)

                @pl.when(at_end)
                def _():
                    part_start(b, g)

            join(g, True)

            @pl.when(closing)
            def _():
                @pl.when(hi > 0)
                def _():
                    absorb(hi, g)

                @pl.when(hi < end)
                def _():
                    absorb(far, g)

                o = acc[0, g] / total[0, g]
                for h in range(per_group):
                    full[hi, g, :, h * hd:(h + 1) * hd] = o[:, h * tok:(h + 1) * tok].T.astype(full.dtype)

                @pl.when(hi < end)
                def _():
                    a_copy(hi, g, hi + 1, 0).start()

                @pl.when(hi > 0)
                def _():
                    a_copy(hi, g, hi - 1, 1).start()

                @pl.when(g == groups - 1)
                def _():
                    pass_w(0)

            @pl.when(jnp.logical_not(at_end))
            def _():
                @pl.when((i < end) & jnp.logical_not(ahead & (i == 0)))
                def _():
                    intake(i + 1, g, jnp.logical_not(rising))

                @pl.when((i == 0) & (g > 0))
                def _():
                    intake(1, g - 1, rising)

                @pl.when((i == 1) & (g == 0))
                def _():
                    intake(1, groups - 1, rising)

                @pl.when((i > 0) & (i < end))
                def _():
                    intake(i + 1, g, rising)

        @pl.when(i == 0)
        def _():
            @pl.loop(2, far)
            def _(k):
                for s in range(sel):
                    plan(order(k), s)

        @pl.when(jnp.logical_not(at_end))
        def _():
            @pl.loop(0, groups)
            def _(g):
                @pl.when((i == hi - 1) & (g >= first(hi)))
                def _():
                    q_copy(hi, g, hi + 1, 0).start()

                @pl.when((i == end - hi - 1) & (g >= first(end - hi)))
                def _():
                    q_copy(hi, g, hi - 1, 1).start()

    def part_copy(z):
        return pltpu.make_async_remote_copy(
            src_ref=part.at[z, 1 - head], dst_ref=got.at[z], send_sem=part_send,
            recv_sem=part_recv.at[z], device_id=mate, device_id_type=MESH)

    def out_copy(z, owner):
        return pltpu.make_async_remote_copy(
            src_ref=low.at[z], dst_ref=out_ref.at[:, pl.ds(pl.multiple_of(owner * wide, wide), wide)],
            send_sem=out_send, recv_sem=out_recv.at[owner], device_id=at(z), device_id_type=MESH)

    keep_copy = pltpu.make_async_copy(
        low.at[hi], out_ref.at[:, pl.ds(pl.multiple_of(hi * wide, wide), wide)], load_sem.at[2])

    def compute(z, j):
        at_j = pl.ds(pl.multiple_of(j * columns, columns), columns)
        terms = jnp.dot(full[z, 0], wv[j, 0:slice_depth], preferred_element_type=jnp.float32)
        for g in range(1, groups):
            terms += jnp.dot(full[z, g], wv[j, g * slice_depth:(g + 1) * slice_depth],
                             preferred_element_type=jnp.float32)
        part[z, 0, :, at_j] = terms[:half]
        part[z, 1, :, at_j] = terms[half:]

    def finish(z):
        part_copy(z).wait_recv()
        rows = (part[z, head] + got[z]).astype(out_ref.dtype)

        low[z] = rows

        @pl.when(z == hi)
        def _():
            keep_copy.start()

        @pl.when(z != hi)
        def _():
            out_copy(z, hi).start()

    load_w.wait()
    settle = min(2, end)

    @pl.loop(0, far)
    def _(d):
        @pl.when(d > 0)
        def _():
            @pl.loop(0, groups)
            def _(g):
                @pl.loop(0, 2)
                def _(turn):
                    above = (turn == 0) == rising

                    @pl.when(jnp.logical_not(above) & (hi - d >= 0))
                    def _():
                        a_copy(hi - d, g, hi, 0).wait_recv()

                        @pl.when(hi < end)
                        def _():
                            a_copy(hi - d, g, hi + 1, 0).start()

                    @pl.when(above & (hi + d <= end))
                    def _():
                        a_copy(hi + d, g, hi, 1).wait_recv()

                        @pl.when(hi > 0)
                        def _():
                            a_copy(hi + d, g, hi - 1, 1).start()

                @pl.when((d == 1) & (g < groups - 1))
                def _():
                    pass_w(g + 1)

        def around(reach, act):
            @pl.loop(0, 2)
            def _(side):
                z = hi + reach * (2 * side - 1)

                @pl.when((z >= 0) & (z < far) & ((reach > 0) | (side == 0)))
                def _():
                    act(z)

        def within(act):
            @pl.loop(0, 2 * settle - 1)
            def _(n):
                z = hi - (settle - 1) + n

                @pl.when((z >= 0) & (z < far))
                def _():
                    act(z)

        def rest(z):
            compute(z, 1 - lo)
            part_copy(z).start()

        @pl.when(d == settle)
        def _():
            rows = pl.ds(pl.multiple_of((1 - grp % 2) * groups * slab, slab), groups * slab)
            pltpu.make_async_remote_copy(
                src_ref=wv.at[1 - lo, rows], dst_ref=wv.at[1 - lo, rows], send_sem=wx_send,
                recv_sem=wx_recv, device_id=twin, device_id_type=MESH).wait_recv()

            within(rest)

        def whole(z):
            compute(z, lo)

            @pl.when(d >= settle)
            def _():
                rest(z)

        around(d, whole)

        @pl.when(d == settle)
        def _():
            within(finish)

        @pl.when(d > settle)
        def _():
            around(d - 1, finish)

        @pl.when(d == end)
        def _():
            around(d, finish)

    def sent(src, sem):
        pltpu.make_async_remote_copy(
            src_ref=src, dst_ref=src, send_sem=sem, recv_sem=load_sem.at[0],
            device_id=mate, device_id_type=MESH).wait_send()

    sent(w_ref.at[pl.ds(0, groups * slab)], wy_send)
    sent(w_ref.at[pl.ds(0, groups * slab)], wx_send)
    sent(gift, kv_send)
    sent(got, part_send)
    sent(low.at[pl.ds(0, end)], out_send)

    @pl.loop(0, far)
    def _(z):
        @pl.when((z <= hi) & (hi < end))
        def _():
            sent(qt.at[z], q_send.at[0, z])
            sent(full.at[z], a_send.at[0, z])

        @pl.when((z >= hi) & (hi > 0))
        def _():
            sent(qt.at[z], q_send.at[1, z])
            sent(full.at[z], a_send.at[1, z])

        @pl.when(z != hi)
        def _():
            sent(mine.at[z], p_send.at[z])
            sent(mine_st.at[z], s_send.at[z])
            out_copy(z, z).wait_recv()

    keep_copy.wait()


def local(queries, new_keys, new_values, cluster_kv, cluster_len, piece_slot, cluster_ids, w_out):
    peers = lax.axis_size("req")
    far = peers // 2
    tok, heads, hd = queries.shape
    piece_keys = cluster_kv.shape[3]
    pieces = piece_slot.shape[1]
    sel = cluster_ids.shape[2]
    count = sel * (pieces // peers)
    groups = min(4, heads)
    cols = heads * tok // groups
    keys = count * piece_keys
    half = tok // lax.axis_size("head")
    depth, columns = w_out.shape
    wide = 2 * columns
    smem = pl.BlockSpec(memory_space=pltpu.SMEM)
    any_space = pl.BlockSpec(memory_space=pltpu.HBM)
    low_type, dma = jnp.bfloat16, pltpu.SemaphoreType.DMA
    return pl.pallas_call(
        functools.partial(serve_kernel, far),
        out_shape=jax.ShapeDtypeStruct((half, peers * columns), low_type),
        in_specs=[smem, smem, smem, any_space, any_space, any_space, any_space, any_space],
        out_specs=any_space,
        scratch_shapes=[
            pltpu.SMEM((2, far, count), jnp.int32),
            pltpu.SMEM((far, count), jnp.int32),
            pltpu.VMEM(cluster_kv.shape, cluster_kv.dtype),
            pltpu.VMEM((far, count, 2, piece_keys, hd), cluster_kv.dtype),
            pltpu.VMEM((hd, tok), low_type),
            pltpu.VMEM(queries.shape, low_type),
            pltpu.VMEM((2, tok, hd), low_type),
            pltpu.VMEM((far, count, 2, piece_keys, hd), cluster_kv.dtype),
            pltpu.VMEM((far, groups, hd, cols), low_type),
            pltpu.VMEM((2, keys, hd), low_type),
            pltpu.VMEM((2, hd, keys), low_type),
            pltpu.VMEM((2, groups, 1, cols), jnp.float32),
            pltpu.VMEM((2, groups, 1, cols), jnp.float32),
            pltpu.VMEM((2, groups, hd, cols), jnp.float32),
            pltpu.VMEM((far, groups, hd, cols), low_type),
            pltpu.VMEM((far, groups, 2, cols), jnp.float32),
            pltpu.VMEM((far + 1, groups, hd, cols), low_type),
            pltpu.VMEM((far + 1, groups, 2, cols), jnp.float32),
            pltpu.VMEM((far, groups, tok, depth // groups), low_type),
            pltpu.VMEM((2, depth, columns), w_out.dtype),
            pltpu.VMEM((far, 2, half, wide), jnp.float32),
            pltpu.VMEM((far, half, wide), jnp.float32),
            pltpu.VMEM((far, half, wide), low_type),
            dma((5,)),
            dma,
            dma((far, 1)),
            dma((2, far)),
            dma((far, groups)),
            dma((far,)),
            dma((far + 1, groups)),
            dma((far,)),
            dma((far + 1, groups)),
            dma((2, far)),
            dma((far, groups)),
            dma,
            dma((groups,)),
            dma,
            dma,
            dma,
            dma((far,)),
            dma,
            dma((far,)),
        ],
        compiler_params=pltpu.CompilerParams(
            collective_id=0, has_side_effects=True, vmem_limit_bytes=50 * 2**20),
        name="serve",
    )(*(pltpu.with_memory_space_constraint(x, pltpu.HBM) for x in (
        cluster_ids[:, 0].T, piece_slot, cluster_len, queries, new_keys[:, 0], new_values[:, 0], cluster_kv, w_out)))


def solution(mesh):
    return jax.shard_map(
        local,
        mesh=mesh,
        in_specs=(
            P(("groups", "req"), "head", None),
            P(("groups", "req"), "head", None),
            P(("groups", "req"), "head", None),
            P(("groups", "req"), "head", None, None, None),
            P("groups"),
            P("groups", None),
            P("groups", "head", None),
            P("head", "req"),
        ),
        out_specs=P(("groups", "req", "head"), None),
        check_vma=False,
    )
```
